128 devices in a mesh: tile: 16 (over x, z_lo, core), member: 8 (over z_hi, y).
Axes of the slice: x: 4, y: 4, z: 4 (z_hi: 2, z_lo: 2; z = z_hi * 2 + z_lo), core: 2. Of those that a mesh axis runs over, the one named last changes fastest.
Arguments:
- residual_in: float32 [64, 256, 1024], P(None, 'tile', 'member'), may hold values from -6 to 6
- members: bfloat16 [16, 64, 256, 1024], P('member', None, 'tile'), may hold values from -6 to 6
- wind_x: float32 [64], replicated, may hold values from 0.05 to 0.25
- wind_y: float32 [64], replicated, may hold values from 0.05 to 0.25
Outputs:
- analysis: float32 [64, 256, 1024], P(None, 'tile', 'member')
- residual: float32 [64, 256, 1024], P(None, 'tile', 'member')
The draws below stay inside these ranges and needn't reach their ends.
All inputs are finite; a program needn't handle non-finite values.
Results may differ from the reference program's by a relative error of at most 0.006.
Values may be sent and summed in bfloat16 or wider, within the bound.
A program may use at most 64 MiB of HBM per device.

```python
import jax
import jax.numpy as jnp
from jax import lax

LEVELS = 64
ITERS = 2
MODEL_STEPS = 4
NX = 256
NY = 1024
MEMBERS = 16


def strengthened(values, rng, source, target, shards_of, factor):
    owner, partner = [(jnp.arange(values.shape[dim]) // (values.shape[dim] // shards_of)).reshape([-1 if axis == dim else 1 for axis in range(values.ndim)]) for dim in (source, target)]
    chosen = jax.random.permutation(rng, shards_of)[partner]
    strong = (owner == chosen) | (owner == (partner + shards_of // 2) % shards_of)
    return jnp.where(strong, factor * values, values)


def block_scale(stream_key, shape, cuts, smallest, largest):
    level, own = 1.0, jax.random.fold_in(stream_key, 6)
    for dim, parts in cuts:
        steps = jnp.exp(jax.random.uniform(jax.random.fold_in(own, dim), (parts,), jnp.float32, smallest / len(cuts), largest / len(cuts)))
        level = level * jnp.repeat(steps, shape[dim] // parts).reshape([-1 if axis == dim else 1 for axis in range(len(shape))])
    return level


def bell_draw(rng, shape, width, most, split=(), kind=jnp.bfloat16):
    level = block_scale(rng, shape, split, -0.22, 0.18) if split else 1.0
    values = jax.random.normal(rng, shape, jnp.float32) * width * level
    return jnp.minimum(jnp.maximum(values, -most), most).astype(kind)


def noise_with(own_key, shape, spread, reach, shards, heavy, kind=jnp.bfloat16):
    values = spread * jax.random.normal(own_key, shape, jnp.float32)
    if shards:
        values = values * block_scale(own_key, shape, shards, -0.22, 0.18)
    return jnp.clip(strengthened(values, jax.random.fold_in(own_key, 3), *heavy), -reach, reach).astype(kind)


def setup_inputs(seed: int = 0) -> dict:
    splits = jax.random.split(jax.random.key(seed), 5)
    return {
        "residual_in": bell_draw(splits[0], (LEVELS, NX, NY), 1.0, 6.0, ((1, 16), (2, 8)), jnp.float32),
        "members": noise_with(splits[1], (MEMBERS, LEVELS, NX, NY), 1.0, 6.0, ((0, 8), (2, 16)), (0, 3, 8, 2.0)),
        "wind_x": jnp.clip(jax.random.uniform(splits[2], (LEVELS,), jnp.float32, 0.05, 0.25), 0.05, 0.25),
        "wind_y": jnp.clip(jax.random.uniform(splits[3], (LEVELS,), jnp.float32, 0.05, 0.25), 0.05, 0.25),
    }


diffusion = 0.1
relax = 0.5


def taper_weights():
    raw = [1.0 - (k / 17.0) ** 2 for k in range(-16, 17)]
    total = sum(raw)
    return [value / total for value in raw]


def adjoint_step(field, wind_x, wind_y):
    padded = jnp.pad(field, ((0, 0), (1, 1), (1, 1)))
    center = padded[:, 1:-1, 1:-1]
    ahead_x = padded[:, 2:, 1:-1]
    behind_x = padded[:, :-2, 1:-1]
    ahead_y = padded[:, 1:-1, 2:]
    behind_y = padded[:, 1:-1, :-2]
    result = center + diffusion * (ahead_x + behind_x + ahead_y + behind_y - 4.0 * center)
    result = result - wind_x[:, None, None] * (center - ahead_x)
    return result - wind_y[:, None, None] * (center - ahead_y)


def smooth_axis(padded, count, axis):
    weights = taper_weights()
    total = weights[0] * lax.slice_in_dim(padded, 0, count, axis=axis)
    for offset in range(1, len(weights)):
        total = total + weights[offset] * lax.slice_in_dim(padded, offset, offset + count, axis=axis)
    return total


def localize(field):
    rows = field.shape[0]
    columns = field.shape[1]
    smoothed = smooth_axis(jnp.pad(field, ((16, 16), (0, 0))), rows, 0)
    return smooth_axis(jnp.pad(smoothed, ((0, 0), (16, 16))), columns, 1)


def reference(residual_in, members, wind_x, wind_y):
    residual = residual_in
    analysis = jnp.zeros_like(residual_in)
    for iteration in range(ITERS):
        field = residual
        for sweep in range(MODEL_STEPS):
            field = adjoint_step(field, wind_x, wind_y)
        grad = field.astype(jnp.bfloat16).astype(jnp.float32)

        def accumulate(carry, member):
            member_f = member.astype(jnp.float32)
            project = jnp.sum(member_f * grad, axis=0)
            localized = localize(project)
            return carry + member_f * localized[None], None

        increment, unused = lax.scan(accumulate, jnp.zeros_like(residual_in), members)
        analysis = analysis + increment
        residual = residual - relax * increment
    return analysis, residual
```

```python
import functools

import jax
import jax.numpy as jnp
from jax import lax
from jax.experimental import pallas as pl
from jax.experimental.pallas import tpu as pltpu
from jax.sharding import PartitionSpec as P

MESH = pl.DeviceIdType.MESH
F32 = jnp.float32
BF16 = jnp.bfloat16

LEV = 64
ROWS = 16
COLS = 128
GROUPS = LEV // 8
STEPS = 4
HALO = STEPS
XROWS = ROWS + 2 * HALO
REACH = 16
CHUNKS = 4
CLEV = LEV // CHUNKS

diffusion = 0.1
relax = 0.5

FLOWS = ((2, 1), (1, 1), (3, 1), (0, 1), (2, 0), (1, 0), (3, 0))
SIDES = ((1, 0), (-1, 0), (0, 1), (0, -1), (1, 1), (-1, 1), (1, -1), (-1, -1))


def taper_weights():
    raw = [1.0 - (k / 17.0) ** 2 for k in range(-16, 17)]
    total = sum(raw)
    return [value / total for value in raw]


def kernel(
    tiles, blocks,
    res_hbm, mem_hbm, wx_ref, wy_ref,
    ana_ref,
    res, mt, a0, a1, w1, w2, c0, ax, ay, own, strip, mr, ml, ql, qr, gt, g,
    proj, sx, pk_r, pk_l, cl, cr, hx, band, z,
    own_sem, res_sem, m_send, m_recv, h_send, h_recv, p_send, p_recv, c_send, c_recv,
):
    t = lax.axis_index("tile")
    m = lax.axis_index("member")
    zh, y = m // 4, m % 4
    w = taper_weights()

    def there(dt, dm):
        ok = None
        for cond in ([t < tiles - 1] if dt > 0 else [t > 0] if dt < 0 else []) + (
            [m < blocks - 1] if dm > 0 else [m > 0] if dm < 0 else []
        ):
            ok = cond if ok is None else jnp.logical_and(ok, cond)
        return ok

    def peer(dt, dm):
        return ((t + dt + tiles) % tiles, (m + dm + blocks) % blocks)

    def mate(dy, dz):
        return ((zh + dz) % 2) * 4 + (y + dy + 4) % 4

    res_copy = pltpu.make_async_copy(res_hbm, res, res_sem)
    res_copy.start()
    own_copy = pltpu.make_async_copy(
        mem_hbm.at[:, :, :, pl.ds(pl.multiple_of(m * COLS, COLS), COLS)], mt.at[m], own_sem
    )
    own_copy.start()

    barrier = pltpu.get_barrier_semaphore()
    count = jnp.int32(len(FLOWS))
    for dy, dz in FLOWS:
        pl.semaphore_signal(barrier, inc=1, device_id=(t, mate(dy, dz)), device_id_type=MESH)
    for dt, dm in SIDES:
        if dt == 0:
            continue
        ok = there(dt, dm)
        count = count + ok.astype(jnp.int32)

        @pl.when(ok)
        def _():
            pl.semaphore_signal(barrier, inc=1, device_id=peer(dt, dm), device_id_type=MESH)

    pl.semaphore_wait(barrier, count)

    def member_copy(i, c):
        dy, dz = FLOWS[i]
        target = mate(dy, dz)
        return pltpu.make_async_remote_copy(
            src_ref=mem_hbm.at[
                :, pl.ds(c * CLEV, CLEV), :, pl.ds(pl.multiple_of(target * COLS, COLS), COLS)
            ],
            dst_ref=mt.at[m, :, pl.ds(c * CLEV, CLEV)],
            send_sem=m_send.at[i, c],
            recv_sem=m_recv.at[i, c],
            device_id=(t, target),
            device_id_type=MESH,
        )

    for i in range(len(FLOWS)):
        member_copy(i, 0).start()

    @pl.when(t == 0)
    def _():
        for a in (a0, a1):
            a[pl.ds(0, HALO * LEV), :] = jnp.zeros((HALO * LEV, COLS), F32)
        ql[:, 0] = jnp.zeros((2, 8, COLS), F32)
        qr[:, 0] = jnp.zeros((2, 8, COLS), F32)
        proj[:, :, 0:REACH, :] = jnp.zeros((2, 16, REACH, COLS), F32)

    @pl.when(t == tiles - 1)
    def _():
        for a in (a0, a1):
            a[pl.ds((HALO + ROWS) * LEV, HALO * LEV), :] = jnp.zeros((HALO * LEV, COLS), F32)
        ql[:, 5] = jnp.zeros((2, 8, COLS), F32)
        qr[:, 5] = jnp.zeros((2, 8, COLS), F32)
        proj[:, :, REACH + ROWS :, :] = jnp.zeros((2, 16, REACH, COLS), F32)

    @pl.when(m == 0)
    def _():
        ql[...] = jnp.zeros(ql.shape, F32)
        cl[...] = jnp.zeros(cl.shape, F32)

    @pl.when(m == blocks - 1)
    def _():
        qr[...] = jnp.zeros(qr.shape, F32)
        cr[...] = jnp.zeros(cr.shape, F32)

    lane = lax.broadcasted_iota(jnp.int32, (8, COLS), 1)
    q = lane % 16
    group = lane // 16

    def quad_copy(it, d):
        a = (a0, a1)[it]
        dt, dm = SIDES[d]
        if dm == 0:
            rows = HALO * LEV
            src = a.at[pl.ds(ROWS * LEV if dt > 0 else HALO * LEV, rows)]
            dst = a.at[pl.ds(0 if dt > 0 else (HALO + ROWS) * LEV, rows)]
        else:
            src, dst = (mr.at[it], ql.at[it]) if dm > 0 else (ml.at[it], qr.at[it])
            if dt == 0:
                src, dst = src, dst.at[pl.ds(1, 4)]
            elif dt > 0:
                src, dst = src.at[pl.ds(3, 1)], dst.at[pl.ds(0, 1)]
            else:
                src, dst = src.at[pl.ds(0, 1)], dst.at[pl.ds(5, 1)]
        return pltpu.make_async_remote_copy(
            src_ref=src, dst_ref=dst, send_sem=h_send.at[it, d], recv_sem=h_recv.at[it, d],
            device_id=peer(dt, dm), device_id_type=MESH,
        )

    def guarded(ok, action):
        if ok is None:
            action()
        else:
            pl.when(ok)(action)

    def edges(a, r):
        total = jnp.zeros((8, COLS), F32)
        for k in range(GROUPS):
            v = a[pl.ds(pl.multiple_of(r * LEV + 8 * k, 8), 8), :]
            low = pltpu.roll(v, (16 * k + 4) % COLS, 1)
            high = pltpu.roll(v, (16 * k + 12) % COLS, 1)
            part = jnp.where(q < 8, low, high)
            total = jnp.where(group == k, part, total)
        return total

    def send_halos(it):
        a = (a0, a1)[it]
        for d in (0, 1):
            guarded(there(*SIDES[d]), quad_copy(it, d).start)

        def pack(r, carry):
            own[HALO + r] = edges(a, HALO + r)
            return carry

        lax.fori_loop(0, ROWS, pack, 0)
        for quad in range(4):
            right = jnp.zeros((8, COLS), F32)
            left = jnp.zeros((8, COLS), F32)
            for k in range(4):
                v = own[HALO + 4 * quad + k]
                here = q // 4 == k
                right = jnp.where(here, pltpu.roll(v, (4 * k - 8) % COLS, 1), right)
                left = jnp.where(here, pltpu.roll(v, (4 * k - 4) % COLS, 1), left)
            mr[it, quad] = right
            ml[it, quad] = left
        for d in range(2, 8):
            guarded(there(*SIDES[d]), quad_copy(it, d).start)

    res_copy.wait()

    def spread(l, carry):
        v = res[l]
        a0[pl.ds(HALO * LEV + l, 8, stride=LEV), :] = v[0:8]
        a0[pl.ds((HALO + 8) * LEV + l, 8, stride=LEV), :] = v[8:16]
        return carry

    lax.fori_loop(0, LEV, spread, 0, unroll=4)
    send_halos(0)
    for c in range(1, CHUNKS):
        for i in range(len(FLOWS)):
            member_copy(i, c).start()

    def coefficients(l, carry):
        wx, wy = wx_ref[l], wy_ref[l]
        c0[pl.ds(l, 1), :] = jnp.full((1, COLS), (1.0 - 4.0 * diffusion - wx - wy) / diffusion, F32)
        ax[pl.ds(l, 1), :] = jnp.full((1, COLS), (diffusion + wx) / diffusion, F32)
        ay[pl.ds(l, 1), :] = jnp.full((1, COLS), (diffusion + wy) / diffusion, F32)
        return carry

    lax.fori_loop(0, LEV, coefficients, 0)

    j = lax.broadcasted_iota(jnp.int32, (2 * COLS, COLS), 0)
    k = jnp.where(j < COLS + COLS // 2, j, j - 2 * COLS) - lax.broadcasted_iota(
        jnp.int32, (2 * COLS, COLS), 1
    )
    total_w = sum(1.0 - (i / 17.0) ** 2 for i in range(-16, 17))
    kf = k.astype(F32)
    full = jnp.where(jnp.abs(k) <= REACH, (1.0 - kf * kf * (1.0 / 289.0)) * (1.0 / total_w), 0.0)
    coarse = full.astype(BF16)
    band[0] = coarse
    band[1] = (full - coarse.astype(F32)).astype(BF16)

    def strip_coefficient(ref):
        total = jnp.zeros((8, COLS), F32)
        for k in range(GROUPS):
            total = jnp.where(group == k, ref[8 * k : 8 * k + 8, :], total)
        return total

    row_low = jnp.where(t > 0, 1.0, 0.0).astype(F32)
    row_high = jnp.where(t < tiles - 1, 1.0, 0.0).astype(F32)
    inside = jnp.logical_and(
        jnp.logical_or(q >= 4, m > 0), jnp.logical_or(q < 12, m < blocks - 1)
    )
    strip_mask = jnp.where(inside, 1.0, 0.0).astype(F32)

    def adjoint(it):
        a = (a0, a1)[it]
        for d in range(8):
            dt, dm = SIDES[d]
            guarded(there(-dt, -dm), quad_copy(it, d).wait_recv)

        def pack(r, carry):
            own[r] = edges(a, r)
            own[r + HALO + ROWS] = edges(a, r + HALO + ROWS)
            return carry

        lax.fori_loop(0, HALO, pack, 0)
        for r in range(XROWS):
            left = pltpu.roll(ql[it, r // 4], (-4 * (r % 4)) % COLS, 1)
            right = pltpu.roll(qr[it, r // 4], (12 - 4 * (r % 4)) % COLS, 1)
            strip[0, r] = jnp.where(q < 4, left, jnp.where(q >= 12, right, own[r]))
        sc0, sax, say = strip_coefficient(c0), strip_coefficient(ax), strip_coefficient(ay)
        for step in range(1, STEPS):
            for r in range(step, XROWS - step):
                v = strip[step - 1, r]
                out = (
                    sc0 * v
                    + (strip[step - 1, r - 1] + pltpu.roll(v, 1, 1))
                    + sax * strip[step - 1, r + 1]
                    + say * pltpu.roll(v, COLS - 1, 1)
                ) * strip_mask
                if r < HALO:
                    out = out * row_low
                elif r >= HALO + ROWS:
                    out = out * row_high
                strip[step, r] = out
        for step in range(1, STEPS + 1):
            src = (a, w1, w2, w1)[step - 1]
            dst = (w1, w2, w1, gt)[step - 1]

            def row(r, carry, scale=None):
                side = strip[step - 1, r]
                for k in range(GROUPS):
                    at = r * LEV + 8 * k
                    here = pl.ds(pl.multiple_of(at, 8), 8)
                    v = src[here, :]
                    up = src[pl.ds(pl.multiple_of(at - LEV, 8), 8), :]
                    down = src[pl.ds(pl.multiple_of(at + LEV, 8), 8), :]
                    left = jnp.where(
                        lane == 0, pltpu.roll(side, (-(16 * k + 3)) % COLS, 1), pltpu.roll(v, 1, 1)
                    )
                    right = jnp.where(
                        lane == COLS - 1,
                        pltpu.roll(side, (COLS - 1 - (16 * k + 12)) % COLS, 1),
                        pltpu.roll(v, COLS - 1, 1),
                    )
                    s = slice(8 * k, 8 * k + 8)
                    out = c0[s, :] * v + (up + left) + ax[s, :] * down + ay[s, :] * right
                    if scale is not None:
                        out = out * scale
                    if step == STEPS:
                        out = (out * diffusion**STEPS).astype(BF16).astype(F32)
                        dst[pl.ds(pl.multiple_of(at - HALO * LEV, 8), 8), :] = out
                    else:
                        dst[here, :] = out
                return carry

            if step < STEPS:
                lax.fori_loop(step, HALO, functools.partial(row, scale=row_low), 0)
            lax.fori_loop(HALO, HALO + ROWS, row, 0)
            if step < STEPS:
                lax.fori_loop(
                    HALO + ROWS, XROWS - step, functools.partial(row, scale=row_high), 0
                )

        def gather(l, carry):
            g[l, 0:8, :] = gt[pl.ds(l, 8, stride=LEV), :]
            g[l, 8:16, :] = gt[pl.ds(8 * LEV + l, 8, stride=LEV), :]
            return carry

        lax.fori_loop(0, LEV, gather, 0, unroll=4)

    own_rows = pl.ds(REACH, ROWS)

    def project(it, pair, first, count, fresh):
        if fresh:
            start = (jnp.zeros((ROWS, COLS), F32), jnp.zeros((ROWS, COLS), F32))
        else:
            start = (proj[it, 2 * pair, own_rows, :], proj[it, 2 * pair + 1, own_rows, :])

        def level(l, sums):
            v = g[l]
            return tuple(s + mt[pair, n, l].astype(F32) * v for n, s in enumerate(sums))

        sums = lax.fori_loop(first, first + count, level, start, unroll=4)
        for n in range(2):
            proj[it, 2 * pair + n, own_rows, :] = sums[n]

    def project_copy(it, pair, slot, d):
        return pltpu.make_async_remote_copy(
            src_ref=proj.at[it, pl.ds(2 * pair, 2), own_rows],
            dst_ref=proj.at[it, pl.ds(2 * pair, 2), pl.ds(0 if d == 0 else REACH + ROWS, REACH)],
            send_sem=p_send.at[it, slot, d], recv_sem=p_recv.at[it, slot, d],
            device_id=peer(*SIDES[d]), device_id_type=MESH,
        )

    pairs = [m] + [mate(-dy, dz) for dy, dz in FLOWS]

    def send_project(it, slot):
        for d in (0, 1):
            guarded(there(*SIDES[d]), project_copy(it, pairs[slot], slot, d).start)

    def smooth_rows(it, slot):
        pair = pairs[slot]
        for d in (0, 1):
            dt, dm = SIDES[d]
            guarded(there(-dt, -dm), project_copy(it, pair, slot, d).wait_recv)
        for n in range(2):
            for half in (0, 8):
                at = REACH + half
                total = w[REACH] * proj[it, 2 * pair + n, pl.ds(at, 8), :]
                for k in range(1, REACH + 1):
                    total = total + w[REACH + k] * (
                        proj[it, 2 * pair + n, pl.ds(at - k, 8), :]
                        + proj[it, 2 * pair + n, pl.ds(at + k, 8), :]
                    )
                sx[pl.ds(pl.multiple_of((2 * pair + n) * ROWS + half, 8), 8), :] = total

    def column_copy(it, d):
        src, dst = (pk_r.at[it], cl.at[it]) if d == 0 else (pk_l.at[it], cr.at[it])
        return pltpu.make_async_remote_copy(
            src_ref=src, dst_ref=dst, send_sem=c_send.at[it, d], recv_sem=c_recv.at[it, d],
            device_id=peer(0, 1 if d == 0 else -1), device_id_type=MESH,
        )

    def split(x):
        high = x.astype(BF16)
        return high, (x - high.astype(F32)).astype(BF16)

    def times(x, part):
        high, low = split(x)
        rows = slice(part * COLS, part * COLS + COLS)
        b_high, b_low = band[0, rows, :], band[1, rows, :]
        dot = functools.partial(jnp.dot, preferred_element_type=F32)
        return dot(high, b_high) + (dot(low, b_high) + dot(high, b_low))

    def smooth_columns(it):
        for part in range(2):
            for half in (0, 8):
                right = jnp.zeros((8, COLS), F32)
                left = jnp.zeros((8, COLS), F32)
                for n in range(8):
                    at = (8 * part + n) * ROWS + half
                    v = sx[at : at + 8, :]
                    right = jnp.where(group == n, pltpu.roll(v, (16 * n - 112) % COLS, 1), right)
                    left = jnp.where(group == n, pltpu.roll(v, 16 * n, 1), left)
                at = part * ROWS + half
                pk_r[it, at : at + 8, :] = right
                pk_l[it, at : at + 8, :] = left
        guarded(there(0, 1), column_copy(it, 0).start)
        guarded(there(0, -1), column_copy(it, 1).start)
        z[...] = times(sx[...], 0)
        guarded(there(0, -1), column_copy(it, 0).wait_recv)
        guarded(there(0, 1), column_copy(it, 1).wait_recv)
        for part in range(2):
            for half in (0, 8):
                at = part * ROWS + half
                from_left = cl[it, at : at + 8, :]
                from_right = cr[it, at : at + 8, :]
                for n in range(8):
                    to = (8 * part + n) * ROWS + half
                    hx[to : to + 8, :] = jnp.where(
                        lane < 16,
                        pltpu.roll(from_right, (-16 * n) % COLS, 1),
                        jnp.where(lane >= 112, pltpu.roll(from_left, (112 - 16 * n) % COLS, 1), 0.0),
                    )
        z[...] = z[...] + times(hx[...], 1)

    def increments(it):
        width = 2

        def levels(step, carry):
            sums = [jnp.zeros((ROWS, COLS), F32) for _ in range(width)]
            for pair in range(8):
                for n in range(2):
                    v = z[pl.ds((2 * pair + n) * ROWS, ROWS), :]
                    for i in range(width):
                        sums[i] = sums[i] + mt[pair, n, width * step + i].astype(F32) * v
            for i in range(width):
                l = width * step + i
                if it == 0:
                    ana_ref[l] = sums[i]
                    v = res[l] - relax * sums[i]
                    a1[pl.ds(HALO * LEV + l, 8, stride=LEV), :] = v[0:8]
                    a1[pl.ds((HALO + 8) * LEV + l, 8, stride=LEV), :] = v[8:16]
                else:
                    ana_ref[l] = ana_ref[l] + sums[i]
            return carry

        lax.fori_loop(0, LEV // width, levels, 0)

    adjoint(0)
    own_copy.wait()
    project(0, pairs[0], 0, LEV, True)
    send_project(0, 0)
    for c in range(CHUNKS):
        for i in range(len(FLOWS)):
            member_copy(i, c).wait_recv()
            project(0, pairs[1 + i], c * CLEV, CLEV, c == 0)
            if c == CHUNKS - 1:
                send_project(0, 1 + i)
    for slot in range(8):
        smooth_rows(0, slot)
    smooth_columns(0)
    increments(0)

    send_halos(1)
    adjoint(1)
    for slot in range(8):
        project(1, pairs[slot], 0, LEV, True)
        send_project(1, slot)
    for slot in range(8):
        smooth_rows(1, slot)
    smooth_columns(1)
    increments(1)

    for c in range(CHUNKS):
        for i in range(len(FLOWS)):
            member_copy(i, c).wait_send()
    for it in range(2):
        for d in range(8):
            guarded(there(*SIDES[d]), quad_copy(it, d).wait_send)
        for slot in range(8):
            for d in (0, 1):
                guarded(there(*SIDES[d]), project_copy(it, pairs[slot], slot, d).wait_send)
        guarded(there(0, 1), column_copy(it, 0).wait_send)
        guarded(there(0, -1), column_copy(it, 1).wait_send)


def per_device(tiles, blocks, residual_in, members, wind_x, wind_y):
    vmem = pltpu.VMEM
    dma = lambda *shape: pltpu.SemaphoreType.DMA(shape)
    anywhere = pl.BlockSpec(memory_space=pl.ANY)
    scalars = pl.BlockSpec(memory_space=pltpu.SMEM)
    extended = vmem((XROWS * LEV, COLS), F32)
    coefficient = vmem((LEV, COLS), F32)
    analysis = pl.pallas_call(
        functools.partial(kernel, tiles, blocks),
        out_shape=jax.ShapeDtypeStruct((LEV, ROWS, COLS), F32),
        in_specs=[anywhere, anywhere, scalars, scalars],
        out_specs=pl.BlockSpec(memory_space=vmem),
        scratch_shapes=[
            vmem((LEV, ROWS, COLS), F32),
            vmem((8, 2, LEV, ROWS, COLS), BF16),
            extended, extended, extended, extended,
            coefficient, coefficient, coefficient,
            vmem((XROWS, 8, COLS), F32),
            vmem((STEPS, XROWS, 8, COLS), F32),
            vmem((2, 4, 8, COLS), F32), vmem((2, 4, 8, COLS), F32),
            vmem((2, 6, 8, COLS), F32), vmem((2, 6, 8, COLS), F32),
            vmem((ROWS * LEV, COLS), F32),
            vmem((LEV, ROWS, COLS), F32),
            vmem((2, 16, ROWS + 2 * REACH, COLS), F32),
            vmem((16 * ROWS, COLS), F32),
            vmem((2, 32, COLS), F32), vmem((2, 32, COLS), F32),
            vmem((2, 32, COLS), F32), vmem((2, 32, COLS), F32),
            vmem((16 * ROWS, COLS), F32),
            vmem((2, 2 * COLS, COLS), BF16),
            vmem((16 * ROWS, COLS), F32),
            pltpu.SemaphoreType.DMA, pltpu.SemaphoreType.DMA,
            dma(len(FLOWS), CHUNKS), dma(len(FLOWS), CHUNKS),
            dma(2, 8), dma(2, 8),
            dma(2, 8, 2), dma(2, 8, 2),
            dma(2, 2), dma(2, 2),
        ],
        compiler_params=pltpu.CompilerParams(collective_id=0, has_side_effects=True),
        name="ensemble_step",
    )(residual_in, members, wind_x, wind_y)
    return (analysis, residual_in - relax * analysis)


def solution(mesh):
    return jax.shard_map(
        functools.partial(per_device, mesh.shape["tile"], mesh.shape["member"]),
        mesh=mesh,
        in_specs=(P(None, "tile", "member"), P("member", None, "tile", None), P(), P()),
        out_specs=(P(None, "tile", "member"), P(None, "tile", "member")),
        check_vma=False,
    )
```

```python
import functools

import jax
import jax.numpy as jnp
from jax import lax
from jax.experimental import pallas as pl
from jax.experimental.pallas import tpu as pltpu
from jax.sharding import PartitionSpec as P

MESH = pl.DeviceIdType.MESH
F32 = jnp.float32
BF16 = jnp.bfloat16

LEV = 64
ROWS = 16
COLS = 128
GROUPS = LEV // 8
STEPS = 4
HALO = STEPS
XROWS = ROWS + 2 * HALO
REACH = 16
CHUNKS = 8
CLEV = LEV // CHUNKS

diffusion = 0.1
relax = 0.5

FLOWS = ((2, 1), (1, 1), (3, 1), (0, 1), (2, 0), (1, 0), (3, 0))
SIDES = ((1, 0), (-1, 0), (0, 1), (0, -1), (1, 1), (-1, 1), (1, -1), (-1, -1))


def taper_weights():
    raw = [1.0 - (k / 17.0) ** 2 for k in range(-16, 17)]
    total = sum(raw)
    return [value / total for value in raw]


def kernel(
    tiles, blocks,
    res_hbm, mem_hbm, wx_ref, wy_ref,
    out_ref,
    res, mt, a0, a1, w1, w2, c0, ax, ay, own, strip, mr, ml, ql, qr, gt, g,
    proj, sx, pk_r, pk_l, cl, cr, hx, band, z,
    own_sem, res_sem, m_send, m_recv, h_send, h_recv, p_send, p_recv, c_send, c_recv,
):
    t = lax.axis_index("tile")
    m = lax.axis_index("member")
    zh, y = m // 4, m % 4
    w = taper_weights()

    def there(dt, dm):
        ok = None
        for cond in ([t < tiles - 1] if dt > 0 else [t > 0] if dt < 0 else []) + (
            [m < blocks - 1] if dm > 0 else [m > 0] if dm < 0 else []
        ):
            ok = cond if ok is None else jnp.logical_and(ok, cond)
        return ok

    def peer(dt, dm):
        return ((t + dt + tiles) % tiles, (m + dm + blocks) % blocks)

    def mate(dy, dz):
        return ((zh + dz) % 2) * 4 + (y + dy + 4) % 4

    res_copy = pltpu.make_async_copy(res_hbm, res, res_sem)
    res_copy.start()
    own_copy = pltpu.make_async_copy(
        mem_hbm.at[:, :, :, pl.ds(pl.multiple_of(m * COLS, COLS), COLS)], mt.at[m], own_sem
    )
    own_copy.start()

    barrier = pltpu.get_barrier_semaphore()
    count = jnp.int32(len(FLOWS))
    for dy, dz in FLOWS:
        pl.semaphore_signal(barrier, inc=1, device_id=(t, mate(dy, dz)), device_id_type=MESH)
    for dt, dm in SIDES:
        if dt == 0:
            continue
        ok = there(dt, dm)
        count = count + ok.astype(jnp.int32)

        @pl.when(ok)
        def _():
            pl.semaphore_signal(barrier, inc=1, device_id=peer(dt, dm), device_id_type=MESH)

    pl.semaphore_wait(barrier, count)

    def member_copy(i, c):
        dy, dz = FLOWS[i]
        target = mate(dy, dz)
        return pltpu.make_async_remote_copy(
            src_ref=mem_hbm.at[
                :, pl.ds(c * CLEV, CLEV), :, pl.ds(pl.multiple_of(target * COLS, COLS), COLS)
            ],
            dst_ref=mt.at[m, :, pl.ds(c * CLEV, CLEV)],
            send_sem=m_send.at[i, c],
            recv_sem=m_recv.at[i, c],
            device_id=(t, target),
            device_id_type=MESH,
        )

    for i in range(len(FLOWS)):
        member_copy(i, 0).start()

    @pl.when(t == 0)
    def _():
        for a in (a0, a1):
            a[pl.ds(0, HALO * LEV), :] = jnp.zeros((HALO * LEV, COLS), F32)
        ql[:, 0] = jnp.zeros((2, 8, COLS), F32)
        qr[:, 0] = jnp.zeros((2, 8, COLS), F32)
        proj[:, :, 0:REACH, :] = jnp.zeros((2, 16, REACH, COLS), F32)

    @pl.when(t == tiles - 1)
    def _():
        for a in (a0, a1):
            a[pl.ds((HALO + ROWS) * LEV, HALO * LEV), :] = jnp.zeros((HALO * LEV, COLS), F32)
        ql[:, 5] = jnp.zeros((2, 8, COLS), F32)
        qr[:, 5] = jnp.zeros((2, 8, COLS), F32)
        proj[:, :, REACH + ROWS :, :] = jnp.zeros((2, 16, REACH, COLS), F32)

    @pl.when(m == 0)
    def _():
        ql[...] = jnp.zeros(ql.shape, F32)
        cl[...] = jnp.zeros(cl.shape, F32)

    @pl.when(m == blocks - 1)
    def _():
        qr[...] = jnp.zeros(qr.shape, F32)
        cr[...] = jnp.zeros(cr.shape, F32)

    lane = lax.broadcasted_iota(jnp.int32, (8, COLS), 1)
    q = lane % 16
    group = lane // 16

    def quad_copy(it, d):
        a = (a0, a1)[it]
        dt, dm = SIDES[d]
        if dm == 0:
            rows = HALO * LEV
            src = a.at[pl.ds(ROWS * LEV if dt > 0 else HALO * LEV, rows)]
            dst = a.at[pl.ds(0 if dt > 0 else (HALO + ROWS) * LEV, rows)]
        else:
            src, dst = (mr.at[it], ql.at[it]) if dm > 0 else (ml.at[it], qr.at[it])
            if dt == 0:
                src, dst = src, dst.at[pl.ds(1, 4)]
            elif dt > 0:
                src, dst = src.at[pl.ds(3, 1)], dst.at[pl.ds(0, 1)]
            else:
                src, dst = src.at[pl.ds(0, 1)], dst.at[pl.ds(5, 1)]
        return pltpu.make_async_remote_copy(
            src_ref=src, dst_ref=dst, send_sem=h_send.at[it, d], recv_sem=h_recv.at[it, d],
            device_id=peer(dt, dm), device_id_type=MESH,
        )

    def guarded(ok, action):
        if ok is None:
            action()
        else:
            pl.when(ok)(action)

    def edges(a, r):
        total = jnp.zeros((8, COLS), F32)
        for k in range(GROUPS):
            v = a[pl.ds(pl.multiple_of(r * LEV + 8 * k, 8), 8), :]
            low = pltpu.roll(v, (16 * k + 4) % COLS, 1)
            high = pltpu.roll(v, (16 * k + 12) % COLS, 1)
            part = jnp.where(q < 8, low, high)
            total = jnp.where(group == k, part, total)
        return total

    def send_halos(it):
        a = (a0, a1)[it]
        for d in (0, 1):
            guarded(there(*SIDES[d]), quad_copy(it, d).start)

        def pack(r, carry):
            own[HALO + r] = edges(a, HALO + r)
            return carry

        lax.fori_loop(0, ROWS, pack, 0, unroll=8 if it else 2)
        for quad in range(4):
            right = jnp.zeros((8, COLS), F32)
            left = jnp.zeros((8, COLS), F32)
            for k in range(4):
                v = own[HALO + 4 * quad + k]
                here = q // 4 == k
                right = jnp.where(here, pltpu.roll(v, (4 * k - 8) % COLS, 1), right)
                left = jnp.where(here, pltpu.roll(v, (4 * k - 4) % COLS, 1), left)
            mr[it, quad] = right
            ml[it, quad] = left
        for d in range(2, 8):
            guarded(there(*SIDES[d]), quad_copy(it, d).start)

    res_copy.wait()

    def spread(l, carry):
        v = res[l]
        a0[pl.ds(HALO * LEV + l, 8, stride=LEV), :] = v[0:8]
        a0[pl.ds((HALO + 8) * LEV + l, 8, stride=LEV), :] = v[8:16]
        return carry

    lax.fori_loop(0, LEV, spread, 0, unroll=4)
    send_halos(0)
    for c in range(1, CHUNKS):
        for i in range(len(FLOWS)):
            member_copy(i, c).start()

    def coefficients(l, carry):
        wx, wy = wx_ref[l], wy_ref[l]
        c0[pl.ds(l, 1), :] = jnp.full((1, COLS), (1.0 - 4.0 * diffusion - wx - wy) / diffusion, F32)
        ax[pl.ds(l, 1), :] = jnp.full((1, COLS), (diffusion + wx) / diffusion, F32)
        ay[pl.ds(l, 1), :] = jnp.full((1, COLS), (diffusion + wy) / diffusion, F32)
        return carry

    lax.fori_loop(0, LEV, coefficients, 0)

    j = lax.broadcasted_iota(jnp.int32, (2 * COLS, COLS), 0)
    k = jnp.where(j < COLS + COLS // 2, j, j - 2 * COLS) - lax.broadcasted_iota(
        jnp.int32, (2 * COLS, COLS), 1
    )
    total_w = sum(1.0 - (i / 17.0) ** 2 for i in range(-16, 17))
    kf = k.astype(F32)
    full = jnp.where(jnp.abs(k) <= REACH, (1.0 - kf * kf * (1.0 / 289.0)) * (1.0 / total_w), 0.0)
    coarse = full.astype(BF16)
    band[0] = coarse
    band[1] = (full - coarse.astype(F32)).astype(BF16)

    def strip_coefficient(ref):
        total = jnp.zeros((8, COLS), F32)
        for k in range(GROUPS):
            total = jnp.where(group == k, ref[8 * k : 8 * k + 8, :], total)
        return total

    row_low = jnp.where(t > 0, 1.0, 0.0).astype(F32)
    row_high = jnp.where(t < tiles - 1, 1.0, 0.0).astype(F32)
    inside = jnp.logical_and(
        jnp.logical_or(q >= 4, m > 0), jnp.logical_or(q < 12, m < blocks - 1)
    )
    strip_mask = jnp.where(inside, 1.0, 0.0).astype(F32)

    def adjoint(it):
        a = (a0, a1)[it]
        for d in range(8):
            dt, dm = SIDES[d]
            guarded(there(-dt, -dm), quad_copy(it, d).wait_recv)

        def pack(r, carry):
            own[r] = edges(a, r)
            own[r + HALO + ROWS] = edges(a, r + HALO + ROWS)
            return carry

        lax.fori_loop(0, HALO, pack, 0, unroll=HALO if it else 1)
        for r in range(XROWS):
            left = pltpu.roll(ql[it, r // 4], (-4 * (r % 4)) % COLS, 1)
            right = pltpu.roll(qr[it, r // 4], (12 - 4 * (r % 4)) % COLS, 1)
            strip[0, r] = jnp.where(q < 4, left, jnp.where(q >= 12, right, own[r]))
        sc0, sax, say = strip_coefficient(c0), strip_coefficient(ax), strip_coefficient(ay)
        for step in range(1, STEPS):
            for r in range(step, XROWS - step):
                v = strip[step - 1, r]
                out = (
                    sc0 * v
                    + (strip[step - 1, r - 1] + pltpu.roll(v, 1, 1))
                    + sax * strip[step - 1, r + 1]
                    + say * pltpu.roll(v, COLS - 1, 1)
                ) * strip_mask
                if r < HALO:
                    out = out * row_low
                elif r >= HALO + ROWS:
                    out = out * row_high
                strip[step, r] = out
        for step in range(1, STEPS + 1):
            src = (a, w1, w2, w1)[step - 1]
            dst = (w1, w2, w1, gt)[step - 1]

            def row(r, carry, scale=None):
                side = strip[step - 1, r]
                for k in range(GROUPS):
                    at = r * LEV + 8 * k
                    here = pl.ds(pl.multiple_of(at, 8), 8)
                    v = src[here, :]
                    up = src[pl.ds(pl.multiple_of(at - LEV, 8), 8), :]
                    down = src[pl.ds(pl.multiple_of(at + LEV, 8), 8), :]
                    left = jnp.where(
                        lane == 0, pltpu.roll(side, (-(16 * k + 3)) % COLS, 1), pltpu.roll(v, 1, 1)
                    )
                    right = jnp.where(
                        lane == COLS - 1,
                        pltpu.roll(side, (COLS - 1 - (16 * k + 12)) % COLS, 1),
                        pltpu.roll(v, COLS - 1, 1),
                    )
                    s = slice(8 * k, 8 * k + 8)
                    out = c0[s, :] * v + (up + left) + ax[s, :] * down + ay[s, :] * right
                    if scale is not None:
                        out = out * scale
                    if step == STEPS:
                        out = (out * diffusion**STEPS).astype(BF16).astype(F32)
                        dst[pl.ds(pl.multiple_of(at - HALO * LEV, 8), 8), :] = out
                    else:
                        dst[here, :] = out
                return carry

            if step < STEPS:
                lax.fori_loop(
                    step, HALO, functools.partial(row, scale=row_low), 0, unroll=True if it else 1
                )
            lax.fori_loop(HALO, HALO + ROWS, row, 0, unroll=ROWS if it else 2)
            if step < STEPS:
                lax.fori_loop(
                    HALO + ROWS, XROWS - step, functools.partial(row, scale=row_high), 0,
                    unroll=True if it else 1,
                )

        def gather(l, carry):
            g[l, 0:8, :] = gt[pl.ds(l, 8, stride=LEV), :]
            g[l, 8:16, :] = gt[pl.ds(8 * LEV + l, 8, stride=LEV), :]
            return carry

        lax.fori_loop(0, LEV, gather, 0, unroll=4)

    own_rows = pl.ds(REACH, ROWS)

    def project(it, pair, first, count, fresh):
        if fresh:
            start = (jnp.zeros((ROWS, COLS), F32), jnp.zeros((ROWS, COLS), F32))
        else:
            start = (proj[it, 2 * pair, own_rows, :], proj[it, 2 * pair + 1, own_rows, :])

        def level(l, sums):
            v = g[l]
            return tuple(s + mt[pair, n, l].astype(F32) * v for n, s in enumerate(sums))

        sums = lax.fori_loop(first, first + count, level, start, unroll=4)
        for n in range(2):
            proj[it, 2 * pair + n, own_rows, :] = sums[n]

    def project_copy(it, pair, slot, d):
        return pltpu.make_async_remote_copy(
            src_ref=proj.at[it, pl.ds(2 * pair, 2), own_rows],
            dst_ref=proj.at[it, pl.ds(2 * pair, 2), pl.ds(0 if d == 0 else REACH + ROWS, REACH)],
            send_sem=p_send.at[it, slot, d], recv_sem=p_recv.at[it, slot, d],
            device_id=peer(*SIDES[d]), device_id_type=MESH,
        )

    pairs = [m] + [mate(-dy, dz) for dy, dz in FLOWS]

    def send_project(it, slot):
        for d in (0, 1):
            guarded(there(*SIDES[d]), project_copy(it, pairs[slot], slot, d).start)

    def smooth_rows(it, slot):
        pair = pairs[slot]
        for d in (0, 1):
            dt, dm = SIDES[d]
            guarded(there(-dt, -dm), project_copy(it, pair, slot, d).wait_recv)
        for n in range(2):
            for half in (0, 8):
                at = REACH + half
                total = w[REACH] * proj[it, 2 * pair + n, pl.ds(at, 8), :]
                for k in range(1, REACH + 1):
                    total = total + w[REACH + k] * (
                        proj[it, 2 * pair + n, pl.ds(at - k, 8), :]
                        + proj[it, 2 * pair + n, pl.ds(at + k, 8), :]
                    )
                sx[pl.ds(pl.multiple_of((2 * pair + n) * ROWS + half, 8), 8), :] = total

    def column_copy(it, d):
        src, dst = (pk_r.at[it], cl.at[it]) if d == 0 else (pk_l.at[it], cr.at[it])
        return pltpu.make_async_remote_copy(
            src_ref=src, dst_ref=dst, send_sem=c_send.at[it, d], recv_sem=c_recv.at[it, d],
            device_id=peer(0, 1 if d == 0 else -1), device_id_type=MESH,
        )

    def split(x):
        high = x.astype(BF16)
        return high, (x - high.astype(F32)).astype(BF16)

    def times(x, part):
        high, low = split(x)
        rows = slice(part * COLS, part * COLS + COLS)
        b_high, b_low = band[0, rows, :], band[1, rows, :]
        dot = functools.partial(jnp.dot, preferred_element_type=F32)
        return dot(high, b_high) + (dot(low, b_high) + dot(high, b_low))

    def smooth_columns(it):
        for part in range(2):
            for half in (0, 8):
                right = jnp.zeros((8, COLS), F32)
                left = jnp.zeros((8, COLS), F32)
                for n in range(8):
                    at = (8 * part + n) * ROWS + half
                    v = sx[at : at + 8, :]
                    right = jnp.where(group == n, pltpu.roll(v, (16 * n - 112) % COLS, 1), right)
                    left = jnp.where(group == n, pltpu.roll(v, 16 * n, 1), left)
                at = part * ROWS + half
                pk_r[it, at : at + 8, :] = right
                pk_l[it, at : at + 8, :] = left
        guarded(there(0, 1), column_copy(it, 0).start)
        guarded(there(0, -1), column_copy(it, 1).start)
        z[...] = times(sx[...], 0)
        guarded(there(0, -1), column_copy(it, 0).wait_recv)
        guarded(there(0, 1), column_copy(it, 1).wait_recv)
        for part in range(2):
            for half in (0, 8):
                at = part * ROWS + half
                from_left = cl[it, at : at + 8, :]
                from_right = cr[it, at : at + 8, :]
                for n in range(8):
                    to = (8 * part + n) * ROWS + half
                    hx[to : to + 8, :] = jnp.where(
                        lane < 16,
                        pltpu.roll(from_right, (-16 * n) % COLS, 1),
                        jnp.where(lane >= 112, pltpu.roll(from_left, (112 - 16 * n) % COLS, 1), 0.0),
                    )
        z[...] = z[...] + times(hx[...], 1)

    def increments(it):
        width = 2

        def levels(step, carry):
            sums = [jnp.zeros((ROWS, COLS), F32) for _ in range(width)]
            for pair in range(8):
                for n in range(2):
                    v = z[pl.ds((2 * pair + n) * ROWS, ROWS), :]
                    for i in range(width):
                        sums[i] = sums[i] + mt[pair, n, width * step + i].astype(F32) * v
            for i in range(width):
                l = width * step + i
                if it == 0:
                    half = relax * sums[i]
                    out_ref[l] = half
                    v = res[l] - half
                    a1[pl.ds(HALO * LEV + l, 8, stride=LEV), :] = v[0:8]
                    a1[pl.ds((HALO + 8) * LEV + l, 8, stride=LEV), :] = v[8:16]
                else:
                    out_ref[l] = out_ref[l] + relax * sums[i]
            return carry

        lax.fori_loop(0, LEV // width, levels, 0)

    adjoint(0)
    own_copy.wait()
    project(0, pairs[0], 0, LEV, True)
    send_project(0, 0)
    for c in range(CHUNKS):
        for i in range(len(FLOWS)):
            member_copy(i, c).wait_recv()
            project(0, pairs[1 + i], c * CLEV, CLEV, c == 0)
            if c == CHUNKS - 1:
                send_project(0, 1 + i)
    for slot in range(8):
        smooth_rows(0, slot)
    smooth_columns(0)
    increments(0)

    send_halos(1)
    adjoint(1)
    for slot in range(8):
        project(1, pairs[slot], 0, LEV, True)
        send_project(1, slot)
    for slot in range(8):
        smooth_rows(1, slot)
    smooth_columns(1)
    increments(1)

    for c in range(CHUNKS):
        for i in range(len(FLOWS)):
            member_copy(i, c).wait_send()
    for it in range(2):
        for d in range(8):
            guarded(there(*SIDES[d]), quad_copy(it, d).wait_send)
        for slot in range(8):
            for d in (0, 1):
                guarded(there(*SIDES[d]), project_copy(it, pairs[slot], slot, d).wait_send)
        guarded(there(0, 1), column_copy(it, 0).wait_send)
        guarded(there(0, -1), column_copy(it, 1).wait_send)


def per_device(tiles, blocks, residual_in, members, wind_x, wind_y):
    vmem = pltpu.VMEM
    dma = lambda *shape: pltpu.SemaphoreType.DMA(shape)
    anywhere = pl.BlockSpec(memory_space=pl.ANY)
    scalars = pl.BlockSpec(memory_space=pltpu.SMEM)
    extended = vmem((XROWS * LEV, COLS), F32)
    coefficient = vmem((LEV, COLS), F32)
    half = pl.pallas_call(
        functools.partial(kernel, tiles, blocks),
        out_shape=jax.ShapeDtypeStruct((LEV, ROWS, COLS), F32),
        in_specs=[anywhere, anywhere, scalars, scalars],
        out_specs=pl.BlockSpec(memory_space=vmem),
        scratch_shapes=[
            vmem((LEV, ROWS, COLS), F32),
            vmem((8, 2, LEV, ROWS, COLS), BF16),
            extended, extended, extended, extended,
            coefficient, coefficient, coefficient,
            vmem((XROWS, 8, COLS), F32),
            vmem((STEPS, XROWS, 8, COLS), F32),
            vmem((2, 4, 8, COLS), F32), vmem((2, 4, 8, COLS), F32),
            vmem((2, 6, 8, COLS), F32), vmem((2, 6, 8, COLS), F32),
            vmem((ROWS * LEV, COLS), F32),
            vmem((LEV, ROWS, COLS), F32),
            vmem((2, 16, ROWS + 2 * REACH, COLS), F32),
            vmem((16 * ROWS, COLS), F32),
            vmem((2, 32, COLS), F32), vmem((2, 32, COLS), F32),
            vmem((2, 32, COLS), F32), vmem((2, 32, COLS), F32),
            vmem((16 * ROWS, COLS), F32),
            vmem((2, 2 * COLS, COLS), BF16),
            vmem((16 * ROWS, COLS), F32),
            pltpu.SemaphoreType.DMA, pltpu.SemaphoreType.DMA,
            dma(len(FLOWS), CHUNKS), dma(len(FLOWS), CHUNKS),
            dma(2, 8), dma(2, 8),
            dma(2, 8, 2), dma(2, 8, 2),
            dma(2, 2), dma(2, 2),
        ],
        compiler_params=pltpu.CompilerParams(collective_id=0, has_side_effects=True),
        name="ensemble_step",
    )(residual_in, members, wind_x, wind_y)
    return (half * (1.0 / relax), residual_in - half)


def solution(mesh):
    return jax.shard_map(
        functools.partial(per_device, mesh.shape["tile"], mesh.shape["member"]),
        mesh=mesh,
        in_specs=(P(None, "tile", "member"), P("member", None, "tile", None), P(), P()),
        out_specs=(P(None, "tile", "member"), P(None, "tile", "member")),
        check_vma=False,
    )
```

```python
import functools

import jax
import jax.numpy as jnp
from jax import lax
from jax.experimental import pallas as pl
from jax.experimental.pallas import tpu as pltpu
from jax.sharding import PartitionSpec as P

MESH = pl.DeviceIdType.MESH
F32 = jnp.float32
BF16 = jnp.bfloat16

LEV = 64
ROWS = 16
COLS = 128
GROUPS = LEV // 8
STEPS = 4
HALO = STEPS
XROWS = ROWS + 2 * HALO
REACH = 16
CHUNKS = 8
CLEV = LEV // CHUNKS

diffusion = 0.1
relax = 0.5

FLOWS = ((1, 1), (3, 1), (0, 1), (2, 1), (1, 0), (3, 0), (2, 0))
SIDES = ((1, 0), (-1, 0), (0, 1), (0, -1), (1, 1), (-1, 1), (1, -1), (-1, -1))


COLUMN_SIDES = ((1, 1), (-1, 1), (1, -1), (-1, -1), (0, 1), (0, -1))


def taper_weights():
    raw = [1.0 - (k / 17.0) ** 2 for k in range(-16, 17)]
    total = sum(raw)
    return [value / total for value in raw]


def kernel(
    tiles, blocks,
    res_hbm, mem_hbm, wx_hbm, wy_hbm,
    out_ref,
    res, mt, a0, a1, w1, w2, c0, ax, ay, own, strip, sides, mr, ml, ql, qr, gt, g,
    proj, sx, pk_r, pk_l, cl, cr, hx, band, z,
    wx_ref, wy_ref, own_sem, res_sem, wind_sem, m_send, m_recv, h_send, h_recv, p_send, p_recv, c_send, c_recv,
):
    t = lax.axis_index("tile")
    m = lax.axis_index("member")
    zh, y = m // 4, m % 4
    w = taper_weights()

    def there(dt, dm):
        ok = None
        for cond in ([t < tiles - 1] if dt > 0 else [t > 0] if dt < 0 else []) + (
            [m < blocks - 1] if dm > 0 else [m > 0] if dm < 0 else []
        ):
            ok = cond if ok is None else jnp.logical_and(ok, cond)
        return ok

    def peer(dt, dm):
        return ((t + dt + tiles) % tiles, (m + dm + blocks) % blocks)

    def mate(dy, dz):
        return ((zh + dz) % 2) * 4 + (y + dy + 4) % 4

    res_copy = pltpu.make_async_copy(res_hbm, res, res_sem)
    res_copy.start()
    wind_copies = [
        pltpu.make_async_copy(wind, wind_ref, wind_sem.at[n])
        for n, (wind, wind_ref) in enumerate(((wx_hbm, wx_ref), (wy_hbm, wy_ref)))
    ]
    for copy in wind_copies:
        copy.start()
    own_copy = pltpu.make_async_copy(
        mem_hbm.at[:, :, :, pl.ds(pl.multiple_of(m * COLS, COLS), COLS)], mt.at[m], own_sem
    )
    own_copy.start()

    barrier = pltpu.get_barrier_semaphore()
    count = jnp.int32(len(FLOWS))
    for dy, dz in FLOWS:
        pl.semaphore_signal(barrier, inc=1, device_id=(t, mate(dy, dz)), device_id_type=MESH)
    for dt, dm in SIDES:
        if dt == 0:
            continue
        ok = there(dt, dm)
        count = count + ok.astype(jnp.int32)

        @pl.when(ok)
        def _():
            pl.semaphore_signal(barrier, inc=1, device_id=peer(dt, dm), device_id_type=MESH)

    pl.semaphore_wait(barrier, count)

    def member_copy(i, c):
        dy, dz = FLOWS[i]
        target = mate(dy, dz)
        return pltpu.make_async_remote_copy(
            src_ref=mem_hbm.at[
                :, pl.ds(c * CLEV, CLEV), :, pl.ds(pl.multiple_of(target * COLS, COLS), COLS)
            ],
            dst_ref=mt.at[m, :, pl.ds(c * CLEV, CLEV)],
            send_sem=m_send.at[i, c],
            recv_sem=m_recv.at[i, c],
            device_id=(t, target),
            device_id_type=MESH,
        )

    for i in range(len(FLOWS)):
        member_copy(i, 0).start()

    @pl.when(t == 0)
    def _():
        for a in (a0, a1):
            a[pl.ds(0, HALO * LEV), :] = jnp.zeros((HALO * LEV, COLS), F32)
        ql[:, 0] = jnp.zeros((2, 8, COLS), F32)
        qr[:, 0] = jnp.zeros((2, 8, COLS), F32)
        proj[:, :, 0:REACH, :] = jnp.zeros((2, 16, REACH, COLS), F32)
        cl[:, :, 0:REACH, :] = jnp.zeros((2, 2, REACH, COLS), F32)
        cr[:, :, 0:REACH, :] = jnp.zeros((2, 2, REACH, COLS), F32)

    @pl.when(t == tiles - 1)
    def _():
        for a in (a0, a1):
            a[pl.ds((HALO + ROWS) * LEV, HALO * LEV), :] = jnp.zeros((HALO * LEV, COLS), F32)
        ql[:, 5] = jnp.zeros((2, 8, COLS), F32)
        qr[:, 5] = jnp.zeros((2, 8, COLS), F32)
        proj[:, :, REACH + ROWS :, :] = jnp.zeros((2, 16, REACH, COLS), F32)
        cl[:, :, REACH + ROWS :, :] = jnp.zeros((2, 2, REACH, COLS), F32)
        cr[:, :, REACH + ROWS :, :] = jnp.zeros((2, 2, REACH, COLS), F32)

    @pl.when(m == 0)
    def _():
        ql[...] = jnp.zeros(ql.shape, F32)
        cl[...] = jnp.zeros(cl.shape, F32)

    @pl.when(m == blocks - 1)
    def _():
        qr[...] = jnp.zeros(qr.shape, F32)
        cr[...] = jnp.zeros(cr.shape, F32)

    lane = lax.broadcasted_iota(jnp.int32, (8, COLS), 1)
    q = lane % 16
    group = lane // 16

    def quad_copy(it, d):
        a = (a0, a1)[it]
        dt, dm = SIDES[d]
        if dm == 0:
            rows = HALO * LEV
            src = a.at[pl.ds(ROWS * LEV if dt > 0 else HALO * LEV, rows)]
            dst = a.at[pl.ds(0 if dt > 0 else (HALO + ROWS) * LEV, rows)]
        else:
            src, dst = (mr.at[it], ql.at[it]) if dm > 0 else (ml.at[it], qr.at[it])
            if dt == 0:
                src, dst = src, dst.at[pl.ds(1, 4)]
            elif dt > 0:
                src, dst = src.at[pl.ds(3, 1)], dst.at[pl.ds(0, 1)]
            else:
                src, dst = src.at[pl.ds(0, 1)], dst.at[pl.ds(5, 1)]
        return pltpu.make_async_remote_copy(
            src_ref=src, dst_ref=dst, send_sem=h_send.at[it, d], recv_sem=h_recv.at[it, d],
            device_id=peer(dt, dm), device_id_type=MESH,
        )

    def guarded(ok, action):
        if ok is None:
            action()
        else:
            pl.when(ok)(action)

    def edges(a, r):
        total = jnp.zeros((8, COLS), F32)
        for k in range(GROUPS):
            v = a[pl.ds(pl.multiple_of(r * LEV + 8 * k, 8), 8), :]
            low = pltpu.roll(v, (16 * k + 4) % COLS, 1)
            high = pltpu.roll(v, (16 * k + 12) % COLS, 1)
            part = jnp.where(q < 8, low, high)
            total = jnp.where(group == k, part, total)
        return total

    def send_halos(it):
        a = (a0, a1)[it]
        for d in (0, 1):
            guarded(there(*SIDES[d]), quad_copy(it, d).start)

        def pack(r, carry):
            own[HALO + r] = edges(a, HALO + r)
            return carry

        lax.fori_loop(0, ROWS, pack, 0, unroll=8 if it else 2)
        for quad in range(4):
            right = jnp.zeros((8, COLS), F32)
            left = jnp.zeros((8, COLS), F32)
            for k in range(4):
                v = own[HALO + 4 * quad + k]
                here = q // 4 == k
                right = jnp.where(here, pltpu.roll(v, (4 * k - 8) % COLS, 1), right)
                left = jnp.where(here, pltpu.roll(v, (4 * k - 4) % COLS, 1), left)
            mr[it, quad] = right
            ml[it, quad] = left
        for d in range(2, 8):
            guarded(there(*SIDES[d]), quad_copy(it, d).start)

    res_copy.wait()

    def spread(l, carry):
        v = res[l]
        a0[pl.ds(HALO * LEV + l, 8, stride=LEV), :] = v[0:8]
        a0[pl.ds((HALO + 8) * LEV + l, 8, stride=LEV), :] = v[8:16]
        return carry

    lax.fori_loop(0, LEV, spread, 0, unroll=4)
    send_halos(0)
    for c in range(1, CHUNKS):
        for i in range(len(FLOWS)):
            member_copy(i, c).start()

    for copy in wind_copies:
        copy.wait()

    def coefficients(l, carry):
        wx, wy = wx_ref[l], wy_ref[l]
        c0[pl.ds(l, 1), :] = jnp.full((1, COLS), (1.0 - 4.0 * diffusion - wx - wy) / diffusion, F32)
        ax[pl.ds(l, 1), :] = jnp.full((1, COLS), (diffusion + wx) / diffusion, F32)
        ay[pl.ds(l, 1), :] = jnp.full((1, COLS), (diffusion + wy) / diffusion, F32)
        return carry

    lax.fori_loop(0, LEV, coefficients, 0)

    j = lax.broadcasted_iota(jnp.int32, (2 * COLS, COLS), 0)
    k = jnp.where(j < COLS + COLS // 2, j, j - 2 * COLS) - lax.broadcasted_iota(
        jnp.int32, (2 * COLS, COLS), 1
    )
    total_w = sum(1.0 - (i / 17.0) ** 2 for i in range(-16, 17))
    kf = k.astype(F32)
    full = jnp.where(jnp.abs(k) <= REACH, (1.0 - kf * kf * (1.0 / 289.0)) * (1.0 / total_w), 0.0)
    coarse = full.astype(BF16)
    band[0] = coarse
    band[1] = (full - coarse.astype(F32)).astype(BF16)

    def strip_coefficient(ref):
        total = jnp.zeros((8, COLS), F32)
        for k in range(GROUPS):
            total = jnp.where(group == k, ref[8 * k : 8 * k + 8, :], total)
        return total

    row_low = jnp.where(t > 0, 1.0, 0.0).astype(F32)
    row_high = jnp.where(t < tiles - 1, 1.0, 0.0).astype(F32)
    inside = jnp.logical_and(
        jnp.logical_or(q >= 4, m > 0), jnp.logical_or(q < 12, m < blocks - 1)
    )
    strip_mask = jnp.where(inside, 1.0, 0.0).astype(F32)

    def adjoint(it):
        a = (a0, a1)[it]
        for d in range(8):
            dt, dm = SIDES[d]
            guarded(there(-dt, -dm), quad_copy(it, d).wait_recv)

        def pack(r, carry):
            own[r] = edges(a, r)
            own[r + HALO + ROWS] = edges(a, r + HALO + ROWS)
            return carry

        lax.fori_loop(0, HALO, pack, 0, unroll=HALO if it else 1)
        for r in range(XROWS):
            left = pltpu.roll(ql[it, r // 4], (-4 * (r % 4)) % COLS, 1)
            right = pltpu.roll(qr[it, r // 4], (12 - 4 * (r % 4)) % COLS, 1)
            strip[0, r] = jnp.where(q < 4, left, jnp.where(q >= 12, right, own[r]))
        sc0, sax, say = strip_coefficient(c0), strip_coefficient(ax), strip_coefficient(ay)
        for step in range(1, STEPS):
            for r in range(step, XROWS - step):
                v = strip[step - 1, r]
                out = (
                    sc0 * v
                    + (strip[step - 1, r - 1] + pltpu.roll(v, 1, 1))
                    + sax * strip[step - 1, r + 1]
                    + say * pltpu.roll(v, COLS - 1, 1)
                ) * strip_mask
                if r < HALO:
                    out = out * row_low
                elif r >= HALO + ROWS:
                    out = out * row_high
                strip[step, r] = out
        for step in range(STEPS):
            for r in range(step + 1, XROWS - step - 1):
                v = strip[step, r]
                sides[step, r] = jnp.where(
                    q == 0, pltpu.roll(v, COLS - 12, 1), pltpu.roll(v, COLS - 2, 1)
                )
        for step in range(1, STEPS + 1):
            src = (a, w1, w2, w1)[step - 1]
            dst = (w1, w2, w1, gt)[step - 1]

            def row(r, carry, scale=None):
                side = sides[step - 1, r]
                for k in range(GROUPS):
                    at = r * LEV + 8 * k
                    here = pl.ds(pl.multiple_of(at, 8), 8)
                    v = src[here, :]
                    up = src[pl.ds(pl.multiple_of(at - LEV, 8), 8), :]
                    down = src[pl.ds(pl.multiple_of(at + LEV, 8), 8), :]
                    ends = pltpu.roll(side, COLS - 1 - 16 * k, 1)
                    left = jnp.where(lane == 0, ends, pltpu.roll(v, 1, 1))
                    right = jnp.where(lane == COLS - 1, ends, pltpu.roll(v, COLS - 1, 1))
                    s = slice(8 * k, 8 * k + 8)
                    out = c0[s, :] * v + (up + left) + ax[s, :] * down + ay[s, :] * right
                    if scale is not None:
                        out = out * scale
                    if step == STEPS:
                        out = (out * diffusion**STEPS).astype(BF16).astype(F32)
                        dst[pl.ds(pl.multiple_of(at - HALO * LEV, 8), 8), :] = out
                    else:
                        dst[here, :] = out
                return carry

            if step < STEPS:
                lax.fori_loop(
                    step, HALO, functools.partial(row, scale=row_low), 0, unroll=True if it else 1
                )
            lax.fori_loop(HALO, HALO + ROWS, row, 0, unroll=ROWS if it else 2)
            if step < STEPS:
                lax.fori_loop(
                    HALO + ROWS, XROWS - step, functools.partial(row, scale=row_high), 0,
                    unroll=True if it else 1,
                )

        def gather(l, carry):
            g[l, 0:8, :] = gt[pl.ds(l, 8, stride=LEV), :]
            g[l, 8:16, :] = gt[pl.ds(8 * LEV + l, 8, stride=LEV), :]
            return carry

        lax.fori_loop(0, LEV, gather, 0, unroll=4)

    own_rows = pl.ds(REACH, ROWS)

    def project(it, pair, first, count, fresh):
        if fresh:
            start = (jnp.zeros((ROWS, COLS), F32), jnp.zeros((ROWS, COLS), F32))
        else:
            start = (proj[it, 2 * pair, own_rows, :], proj[it, 2 * pair + 1, own_rows, :])

        def level(l, sums):
            v = g[l]
            return tuple(s + mt[pair, n, l].astype(F32) * v for n, s in enumerate(sums))

        sums = lax.fori_loop(first, first + count, level, start, unroll=4)
        for n in range(2):
            proj[it, 2 * pair + n, own_rows, :] = sums[n]

    def project_copy(it, pair, slot, d):
        return pltpu.make_async_remote_copy(
            src_ref=proj.at[it, pl.ds(2 * pair, 2), own_rows],
            dst_ref=proj.at[it, pl.ds(2 * pair, 2), pl.ds(0 if d == 0 else REACH + ROWS, REACH)],
            send_sem=p_send.at[it, slot, d], recv_sem=p_recv.at[it, slot, d],
            device_id=peer(*SIDES[d]), device_id_type=MESH,
        )

    pairs = [m] + [mate(-dy, dz) for dy, dz in FLOWS]

    def send_project(it, slot):
        for d in (0, 1):
            guarded(there(*SIDES[d]), project_copy(it, pairs[slot], slot, d).start)

    def taper(ref, lead, at):
        total = w[REACH] * ref[(*lead, pl.ds(at, 8), slice(None))]
        for k in range(1, REACH + 1):
            total = total + w[REACH + k] * (
                ref[(*lead, pl.ds(at - k, 8), slice(None))]
                + ref[(*lead, pl.ds(at + k, 8), slice(None))]
            )
        return total

    def smooth_rows(it, slot):
        pair = pairs[slot]
        for d in (0, 1):
            dt, dm = SIDES[d]
            guarded(there(-dt, -dm), project_copy(it, pair, slot, d).wait_recv)
        for n in range(2):
            for half in (0, 8):
                sx[pl.ds(pl.multiple_of((2 * pair + n) * ROWS + half, 8), 8), :] = taper(
                    proj, (it, 2 * pair + n), REACH + half
                )

    def column_copy(it, d):
        dt, dm = COLUMN_SIDES[d]
        src, dst = (pk_r.at[it], cl.at[it]) if dm > 0 else (pk_l.at[it], cr.at[it])
        return pltpu.make_async_remote_copy(
            src_ref=src,
            dst_ref=dst.at[:, pl.ds(REACH if dt == 0 else 0 if dt > 0 else REACH + ROWS, ROWS)],
            send_sem=c_send.at[it, d], recv_sem=c_recv.at[it, d],
            device_id=peer(dt, dm), device_id_type=MESH,
        )

    def send_columns(it):
        for part in range(2):
            for half in (0, 8):
                right = jnp.zeros((8, COLS), F32)
                left = jnp.zeros((8, COLS), F32)
                for n in range(8):
                    v = proj[it, 8 * part + n, REACH + half : REACH + half + 8, :]
                    right = jnp.where(group == n, pltpu.roll(v, (16 * n - 112) % COLS, 1), right)
                    left = jnp.where(group == n, pltpu.roll(v, 16 * n, 1), left)
                pk_r[it, part, half : half + 8, :] = right
                pk_l[it, part, half : half + 8, :] = left
        for d, side in enumerate(COLUMN_SIDES):
            guarded(there(*side), column_copy(it, d).start)

    def split(x):
        high = x.astype(BF16)
        return high, (x - high.astype(F32)).astype(BF16)

    def times(x, part):
        high, low = split(x)
        rows = slice(part * COLS, part * COLS + COLS)
        b_high, b_low = band[0, rows, :], band[1, rows, :]
        dot = functools.partial(jnp.dot, preferred_element_type=F32)
        return dot(high, b_high) + (dot(low, b_high) + dot(high, b_low))

    def smooth_columns(it):
        z[...] = times(sx[...], 0)
        for d, (dt, dm) in enumerate(COLUMN_SIDES):
            guarded(there(-dt, -dm), column_copy(it, d).wait_recv)
        for part in range(2):
            for half in (0, 8):
                from_left = taper(cl, (it, part), REACH + half)
                from_right = taper(cr, (it, part), REACH + half)
                for n in range(8):
                    to = (8 * part + n) * ROWS + half
                    hx[to : to + 8, :] = jnp.where(
                        lane < 16,
                        pltpu.roll(from_right, (-16 * n) % COLS, 1),
                        jnp.where(lane >= 112, pltpu.roll(from_left, (112 - 16 * n) % COLS, 1), 0.0),
                    )
        z[...] = z[...] + times(hx[...], 1)

    def increments(it):
        width = 2

        def levels(step, carry):
            sums = [jnp.zeros((ROWS, COLS), F32) for _ in range(width)]
            for pair in range(8):
                for n in range(2):
                    v = z[pl.ds((2 * pair + n) * ROWS, ROWS), :]
                    for i in range(width):
                        sums[i] = sums[i] + mt[pair, n, width * step + i].astype(F32) * v
            for i in range(width):
                l = width * step + i
                if it == 0:
                    half = relax * sums[i]
                    out_ref[l] = half
                    v = res[l] - half
                    a1[pl.ds(HALO * LEV + l, 8, stride=LEV), :] = v[0:8]
                    a1[pl.ds((HALO + 8) * LEV + l, 8, stride=LEV), :] = v[8:16]
                else:
                    out_ref[l] = out_ref[l] + relax * sums[i]
            return carry

        lax.fori_loop(0, LEV // width, levels, 0)

    adjoint(0)
    own_copy.wait()
    project(0, pairs[0], 0, LEV, True)
    send_project(0, 0)
    for c in range(CHUNKS):
        for i in range(len(FLOWS)):
            member_copy(i, c).wait_recv()
            project(0, pairs[1 + i], c * CLEV, CLEV, c == 0)
            if c == CHUNKS - 1:
                send_project(0, 1 + i)
    send_columns(0)
    for slot in range(8):
        smooth_rows(0, slot)
    smooth_columns(0)
    increments(0)

    send_halos(1)
    adjoint(1)
    for slot in range(8):
        project(1, pairs[slot], 0, LEV, True)
        send_project(1, slot)
    send_columns(1)
    for slot in range(8):
        smooth_rows(1, slot)
    smooth_columns(1)
    increments(1)

    for c in range(CHUNKS):
        for i in range(len(FLOWS)):
            member_copy(i, c).wait_send()
    for it in range(2):
        for d in range(8):
            guarded(there(*SIDES[d]), quad_copy(it, d).wait_send)
        for slot in range(8):
            for d in (0, 1):
                guarded(there(*SIDES[d]), project_copy(it, pairs[slot], slot, d).wait_send)
        for d, side in enumerate(COLUMN_SIDES):
            guarded(there(*side), column_copy(it, d).wait_send)


def per_device(tiles, blocks, residual_in, members, wind_x, wind_y):
    vmem = pltpu.VMEM
    dma = lambda *shape: pltpu.SemaphoreType.DMA(shape)
    anywhere = pl.BlockSpec(memory_space=pl.ANY)
    extended = vmem((XROWS * LEV, COLS), F32)
    coefficient = vmem((LEV, COLS), F32)
    half = pl.pallas_call(
        functools.partial(kernel, tiles, blocks),
        out_shape=jax.ShapeDtypeStruct((LEV, ROWS, COLS), F32),
        in_specs=[anywhere] * 4,
        out_specs=pl.BlockSpec(memory_space=vmem),
        scratch_shapes=[
            vmem((LEV, ROWS, COLS), F32),
            vmem((8, 2, LEV, ROWS, COLS), BF16),
            extended, extended, extended, extended,
            coefficient, coefficient, coefficient,
            vmem((XROWS, 8, COLS), F32),
            vmem((STEPS, XROWS, 8, COLS), F32),
            vmem((STEPS, XROWS, 8, COLS), F32),
            vmem((2, 4, 8, COLS), F32), vmem((2, 4, 8, COLS), F32),
            vmem((2, 6, 8, COLS), F32), vmem((2, 6, 8, COLS), F32),
            vmem((ROWS * LEV, COLS), F32),
            vmem((LEV, ROWS, COLS), F32),
            vmem((2, 16, ROWS + 2 * REACH, COLS), F32),
            vmem((16 * ROWS, COLS), F32),
            vmem((2, 2, ROWS, COLS), F32), vmem((2, 2, ROWS, COLS), F32),
            vmem((2, 2, ROWS + 2 * REACH, COLS), F32),
            vmem((2, 2, ROWS + 2 * REACH, COLS), F32),
            vmem((16 * ROWS, COLS), F32),
            vmem((2, 2 * COLS, COLS), BF16),
            vmem((16 * ROWS, COLS), F32),
            pltpu.SMEM((LEV,), F32), pltpu.SMEM((LEV,), F32),
            pltpu.SemaphoreType.DMA, pltpu.SemaphoreType.DMA, dma(2),
            dma(len(FLOWS), CHUNKS), dma(len(FLOWS), CHUNKS),
            dma(2, 8), dma(2, 8),
            dma(2, 8, 2), dma(2, 8, 2),
            dma(2, len(COLUMN_SIDES)), dma(2, len(COLUMN_SIDES)),
        ],
        compiler_params=pltpu.CompilerParams(collective_id=0, has_side_effects=True),
        name="ensemble_step",
    )(residual_in, members, wind_x, wind_y)
    return (half * (1.0 / relax), residual_in - half)


def solution(mesh):
    return jax.shard_map(
        functools.partial(per_device, mesh.shape["tile"], mesh.shape["member"]),
        mesh=mesh,
        in_specs=(P(None, "tile", "member"), P("member", None, "tile", None), P(), P()),
        out_specs=(P(None, "tile", "member"), P(None, "tile", "member")),
        check_vma=False,
    )
```

```python
import functools

import jax
import jax.numpy as jnp
from jax import lax
from jax.experimental import pallas as pl
from jax.experimental.pallas import tpu as pltpu
from jax.sharding import PartitionSpec as P

MESH = pl.DeviceIdType.MESH
F32 = jnp.float32
BF16 = jnp.bfloat16

LEV = 64
ROWS = 16
COLS = 128
GROUPS = LEV // 8
STEPS = 4
HALO = STEPS
XROWS = ROWS + 2 * HALO
REACH = 16
CHUNKS = 8
CLEV = LEV // CHUNKS

diffusion = 0.1
relax = 0.5

FLOWS = ((2, 1), (0, 1), (2, 0), (1, 1), (3, 1), (1, 0), (3, 0))
ORDER = [(i, c) for c in range(CHUNKS) for i in (0, 1, 2)]
ORDER += [(i, c) for c in range(CHUNKS) for i in (3, 4, 5, 6)]
FIRST = 6
HALVES = 2
HLEV = LEV // HALVES
SIDES = ((1, 0), (-1, 0), (0, 1), (0, -1), (1, 1), (-1, 1), (1, -1), (-1, -1))


COLUMN_SIDES = ((1, 1), (-1, 1), (1, -1), (-1, -1), (0, 1), (0, -1))


def taper_weights():
    raw = [1.0 - (k / 17.0) ** 2 for k in range(-16, 17)]
    total = sum(raw)
    return [value / total for value in raw]


def kernel(
    tiles, blocks,
    res_hbm, mem_hbm, wx_hbm, wy_hbm,
    out_ref,
    res, mt, a0, a1, w1, w2, c0, ax, ay, own, strip, sides, mr, ml, ql, qr, gt, g,
    row_out, row_in, proj, proj_out, proj_in, sx, pk_r, pk_l, cl, cr, band, z,
    wx_ref, wy_ref, own_sem, res_sem, wind_sem, m_send, m_recv, h_send, h_recv, r_send, r_recv, p_send, p_recv, c_send, c_recv,
):
    t = lax.axis_index("tile")
    m = lax.axis_index("member")
    zh, y = m // 4, m % 4
    w = taper_weights()

    def there(dt, dm):
        ok = None
        for cond in ([t < tiles - 1] if dt > 0 else [t > 0] if dt < 0 else []) + (
            [m < blocks - 1] if dm > 0 else [m > 0] if dm < 0 else []
        ):
            ok = cond if ok is None else jnp.logical_and(ok, cond)
        return ok

    def peer(dt, dm):
        return ((t + dt + tiles) % tiles, (m + dm + blocks) % blocks)

    def mate(dy, dz):
        return ((zh + dz) % 2) * 4 + (y + dy + 4) % 4

    res_copy = pltpu.make_async_copy(res_hbm, res, res_sem)
    res_copy.start()
    wind_copies = [
        pltpu.make_async_copy(wind, wind_ref, wind_sem.at[n])
        for n, (wind, wind_ref) in enumerate(((wx_hbm, wx_ref), (wy_hbm, wy_ref)))
    ]
    for copy in wind_copies:
        copy.start()
    own_copy = pltpu.make_async_copy(
        mem_hbm.at[:, :, :, pl.ds(pl.multiple_of(m * COLS, COLS), COLS)], mt.at[m], own_sem
    )
    own_copy.start()

    barrier = pltpu.get_barrier_semaphore()
    count = jnp.int32(len(FLOWS))
    for dy, dz in FLOWS:
        pl.semaphore_signal(barrier, inc=1, device_id=(t, mate(dy, dz)), device_id_type=MESH)
    for dt, dm in SIDES:
        if dt == 0:
            continue
        ok = there(dt, dm)
        count = count + ok.astype(jnp.int32)

        @pl.when(ok)
        def _():
            pl.semaphore_signal(barrier, inc=1, device_id=peer(dt, dm), device_id_type=MESH)

    pl.semaphore_wait(barrier, count)

    def member_copy(i, c):
        dy, dz = FLOWS[i]
        target = mate(dy, dz)
        return pltpu.make_async_remote_copy(
            src_ref=mem_hbm.at[
                :, pl.ds(c * CLEV, CLEV), :, pl.ds(pl.multiple_of(target * COLS, COLS), COLS)
            ],
            dst_ref=mt.at[m, :, pl.ds(c * CLEV, CLEV)],
            send_sem=m_send.at[i, c],
            recv_sem=m_recv.at[i, c],
            device_id=(t, target),
            device_id_type=MESH,
        )

    for i, c in ORDER[:FIRST]:
        member_copy(i, c).start()

    @pl.when(t == 0)
    def _():
        for a in (a0, a1):
            a[pl.ds(0, HALO * LEV), :] = jnp.zeros((HALO * LEV, COLS), F32)
        ql[:, 0] = jnp.zeros((2, 8, COLS), F32)
        qr[:, 0] = jnp.zeros((2, 8, COLS), F32)
        proj[:, :, 0:REACH, :] = jnp.zeros((2, 16, REACH, COLS), F32)
        cl[:, :, 0:REACH, :] = jnp.zeros((2, 2, REACH, COLS), F32)
        cr[:, :, 0:REACH, :] = jnp.zeros((2, 2, REACH, COLS), F32)

    @pl.when(t == tiles - 1)
    def _():
        for a in (a0, a1):
            a[pl.ds((HALO + ROWS) * LEV, HALO * LEV), :] = jnp.zeros((HALO * LEV, COLS), F32)
        ql[:, 5] = jnp.zeros((2, 8, COLS), F32)
        qr[:, 5] = jnp.zeros((2, 8, COLS), F32)
        proj[:, :, REACH + ROWS :, :] = jnp.zeros((2, 16, REACH, COLS), F32)
        cl[:, :, REACH + ROWS :, :] = jnp.zeros((2, 2, REACH, COLS), F32)
        cr[:, :, REACH + ROWS :, :] = jnp.zeros((2, 2, REACH, COLS), F32)

    @pl.when(m == 0)
    def _():
        ql[...] = jnp.zeros(ql.shape, F32)
        cl[...] = jnp.zeros(cl.shape, F32)

    @pl.when(m == blocks - 1)
    def _():
        qr[...] = jnp.zeros(qr.shape, F32)
        cr[...] = jnp.zeros(cr.shape, F32)

    lane = lax.broadcasted_iota(jnp.int32, (8, COLS), 1)
    q = lane % 16
    group = lane // 16

    def row_copy(it, d, half):
        return pltpu.make_async_remote_copy(
            src_ref=row_out.at[it, d, half], dst_ref=row_in.at[it, d, half],
            send_sem=r_send.at[it, d, half], recv_sem=r_recv.at[it, d, half],
            device_id=peer(*SIDES[d]), device_id_type=MESH,
        )

    def send_rows(it, half):
        a = (a0, a1)[it]
        for d, first in ((0, ROWS), (1, HALO)):
            for r in range(HALO):
                row_out[it, d, half, r * HLEV : (r + 1) * HLEV, :] = a[
                    (first + r) * LEV + half * HLEV : (first + r) * LEV + (half + 1) * HLEV, :
                ].astype(BF16)
            guarded(there(*SIDES[d]), row_copy(it, d, half).start)

    def receive_rows(it):
        a = (a0, a1)[it]
        for d, first in ((0, 0), (1, HALO + ROWS)):

            def unpack(d=d, first=first):
                for half in range(HALVES):
                    row_copy(it, d, half).wait_recv()
                    for r in range(HALO):
                        at = (first + r) * LEV + half * HLEV
                        a[at : at + HLEV, :] = row_in[
                            it, d, half, r * HLEV : (r + 1) * HLEV, :
                        ].astype(F32)

            dt, dm = SIDES[d]
            guarded(there(-dt, -dm), unpack)

    def quad_copy(it, d):
        dt, dm = SIDES[d]
        src, dst = (mr.at[it], ql.at[it]) if dm > 0 else (ml.at[it], qr.at[it])
        if dt == 0:
            src, dst = src, dst.at[pl.ds(1, 4)]
        elif dt > 0:
            src, dst = src.at[pl.ds(3, 1)], dst.at[pl.ds(0, 1)]
        else:
            src, dst = src.at[pl.ds(0, 1)], dst.at[pl.ds(5, 1)]
        return pltpu.make_async_remote_copy(
            src_ref=src, dst_ref=dst, send_sem=h_send.at[it, d], recv_sem=h_recv.at[it, d],
            device_id=peer(dt, dm), device_id_type=MESH,
        )

    def guarded(ok, action):
        if ok is None:
            action()
        else:
            pl.when(ok)(action)

    def edges(a, r):
        total = jnp.zeros((8, COLS), F32)
        for k in range(GROUPS):
            v = a[pl.ds(pl.multiple_of(r * LEV + 8 * k, 8), 8), :]
            low = pltpu.roll(v, (16 * k + 4) % COLS, 1)
            high = pltpu.roll(v, (16 * k + 12) % COLS, 1)
            part = jnp.where(q < 8, low, high)
            total = jnp.where(group == k, part, total)
        return total

    def send_halos(it):
        a = (a0, a1)[it]

        def pack(r, carry):
            own[HALO + r] = edges(a, HALO + r)
            return carry

        lax.fori_loop(0, ROWS, pack, 0, unroll=8 if it else 2)
        for quad in range(4):
            right = jnp.zeros((8, COLS), F32)
            left = jnp.zeros((8, COLS), F32)
            for k in range(4):
                v = own[HALO + 4 * quad + k]
                here = q // 4 == k
                right = jnp.where(here, pltpu.roll(v, (4 * k - 8) % COLS, 1), right)
                left = jnp.where(here, pltpu.roll(v, (4 * k - 4) % COLS, 1), left)
            mr[it, quad] = right
            ml[it, quad] = left
        for d in range(2, 8):
            guarded(there(*SIDES[d]), quad_copy(it, d).start)

    res_copy.wait()

    def spread(l, carry):
        v = res[l]
        a0[pl.ds(HALO * LEV + l, 8, stride=LEV), :] = v[0:8]
        a0[pl.ds((HALO + 8) * LEV + l, 8, stride=LEV), :] = v[8:16]
        return carry

    lax.fori_loop(0, LEV, spread, 0, unroll=4)
    for half in range(HALVES):
        send_rows(0, half)
    send_halos(0)
    for i, c in ORDER[FIRST:]:
        member_copy(i, c).start()

    for copy in wind_copies:
        copy.wait()

    def coefficients(l, carry):
        wx, wy = wx_ref[l], wy_ref[l]
        c0[pl.ds(l, 1), :] = jnp.full((1, COLS), (1.0 - 4.0 * diffusion - wx - wy) / diffusion, F32)
        ax[pl.ds(l, 1), :] = jnp.full((1, COLS), (diffusion + wx) / diffusion, F32)
        ay[pl.ds(l, 1), :] = jnp.full((1, COLS), (diffusion + wy) / diffusion, F32)
        return carry

    lax.fori_loop(0, LEV, coefficients, 0)

    total_w = sum(1.0 - (i / 17.0) ** 2 for i in range(-16, 17))
    source = lax.broadcasted_iota(jnp.int32, (COLS, COLS), 0)
    target = lax.broadcasted_iota(jnp.int32, (COLS, COLS), 1)
    together = source // 16 == target // 16
    for which, k, near in (
        (0, source - target, None),
        (1, source - 16 - target, together),
        (2, source + 16 - target, together),
    ):
        kf = k.astype(F32)
        reached = jnp.abs(k) <= REACH
        if near is not None:
            reached = jnp.logical_and(reached, near)
        full = jnp.where(reached, (1.0 - kf * kf * (1.0 / 289.0)) * (1.0 / total_w), 0.0)
        coarse = full.astype(BF16)
        band[which, 0] = coarse
        band[which, 1] = (full - coarse.astype(F32)).astype(BF16)

    def strip_coefficient(ref):
        total = jnp.zeros((8, COLS), F32)
        for k in range(GROUPS):
            total = jnp.where(group == k, ref[8 * k : 8 * k + 8, :], total)
        return total

    row_low = jnp.where(t > 0, 1.0, 0.0).astype(F32)
    row_high = jnp.where(t < tiles - 1, 1.0, 0.0).astype(F32)
    inside = jnp.logical_and(
        jnp.logical_or(q >= 4, m > 0), jnp.logical_or(q < 12, m < blocks - 1)
    )
    strip_mask = jnp.where(inside, 1.0, 0.0).astype(F32)

    def adjoint(it):
        a = (a0, a1)[it]
        receive_rows(it)
        for d in range(2, 8):
            dt, dm = SIDES[d]
            guarded(there(-dt, -dm), quad_copy(it, d).wait_recv)

        def pack(r, carry):
            own[r] = edges(a, r)
            own[r + HALO + ROWS] = edges(a, r + HALO + ROWS)
            return carry

        lax.fori_loop(0, HALO, pack, 0, unroll=HALO if it else 1)
        for r in range(XROWS):
            left = pltpu.roll(ql[it, r // 4], (-4 * (r % 4)) % COLS, 1)
            right = pltpu.roll(qr[it, r // 4], (12 - 4 * (r % 4)) % COLS, 1)
            strip[0, r] = jnp.where(q < 4, left, jnp.where(q >= 12, right, own[r]))
        sc0, sax, say = strip_coefficient(c0), strip_coefficient(ax), strip_coefficient(ay)
        for step in range(1, STEPS):
            for r in range(step, XROWS - step):
                v = strip[step - 1, r]
                out = (
                    sc0 * v
                    + (strip[step - 1, r - 1] + pltpu.roll(v, 1, 1))
                    + sax * strip[step - 1, r + 1]
                    + say * pltpu.roll(v, COLS - 1, 1)
                ) * strip_mask
                if r < HALO:
                    out = out * row_low
                elif r >= HALO + ROWS:
                    out = out * row_high
                strip[step, r] = out
        for step in range(STEPS):
            for r in range(step + 1, XROWS - step - 1):
                v = strip[step, r]
                sides[step, r] = jnp.where(
                    q == 0, pltpu.roll(v, COLS - 12, 1), pltpu.roll(v, COLS - 2, 1)
                )
        for step in range(1, STEPS + 1):
            src = (a, w1, w2, w1)[step - 1]
            dst = (w1, w2, w1, gt)[step - 1]

            def row(r, carry, scale=None):
                side = sides[step - 1, r]
                for k in range(GROUPS):
                    at = r * LEV + 8 * k
                    here = pl.ds(pl.multiple_of(at, 8), 8)
                    v = src[here, :]
                    up = src[pl.ds(pl.multiple_of(at - LEV, 8), 8), :]
                    down = src[pl.ds(pl.multiple_of(at + LEV, 8), 8), :]
                    ends = pltpu.roll(side, COLS - 1 - 16 * k, 1)
                    left = jnp.where(lane == 0, ends, pltpu.roll(v, 1, 1))
                    right = jnp.where(lane == COLS - 1, ends, pltpu.roll(v, COLS - 1, 1))
                    s = slice(8 * k, 8 * k + 8)
                    out = c0[s, :] * v + (up + left) + ax[s, :] * down + ay[s, :] * right
                    if scale is not None:
                        out = out * scale
                    if step == STEPS:
                        out = (out * diffusion**STEPS).astype(BF16).astype(F32)
                        dst[pl.ds(pl.multiple_of(at - HALO * LEV, 8), 8), :] = out
                    else:
                        dst[here, :] = out
                return carry

            if step < STEPS:
                lax.fori_loop(
                    step, HALO, functools.partial(row, scale=row_low), 0, unroll=True if it else 1
                )
            lax.fori_loop(HALO, HALO + ROWS, row, 0, unroll=ROWS if it else 2)
            if step < STEPS:
                lax.fori_loop(
                    HALO + ROWS, XROWS - step, functools.partial(row, scale=row_high), 0,
                    unroll=True if it else 1,
                )

        def gather(l, carry):
            g[l, 0:8, :] = gt[pl.ds(l, 8, stride=LEV), :]
            g[l, 8:16, :] = gt[pl.ds(8 * LEV + l, 8, stride=LEV), :]
            return carry

        lax.fori_loop(0, LEV, gather, 0, unroll=4)

    own_rows = pl.ds(REACH, ROWS)

    def project(it, pair, first, count, fresh):
        if fresh:
            start = (jnp.zeros((ROWS, COLS), F32), jnp.zeros((ROWS, COLS), F32))
        else:
            start = (proj[it, 2 * pair, own_rows, :], proj[it, 2 * pair + 1, own_rows, :])

        def level(l, sums):
            v = g[l]
            return tuple(s + mt[pair, n, l].astype(F32) * v for n, s in enumerate(sums))

        sums = lax.fori_loop(first, first + count, level, start, unroll=8)
        for n in range(2):
            proj[it, 2 * pair + n, own_rows, :] = sums[n]

    def project_copy(it, pair, slot, d):
        return pltpu.make_async_remote_copy(
            src_ref=proj_out.at[it, pl.ds(2 * pair, 2)],
            dst_ref=proj_in.at[it, d, pl.ds(2 * pair, 2)],
            send_sem=p_send.at[it, slot, d], recv_sem=p_recv.at[it, slot, d],
            device_id=peer(*SIDES[d]), device_id_type=MESH,
        )

    pairs = [m] + [mate(-dy, dz) for dy, dz in FLOWS]

    def send_project(it, slot):
        for n in range(2):
            member = 2 * pairs[slot] + n
            proj_out[it, member] = proj[it, member, own_rows, :].astype(BF16)
        for d in (0, 1):
            guarded(there(*SIDES[d]), project_copy(it, pairs[slot], slot, d).start)

    def taper(ref, lead, at):
        total = w[REACH] * ref[(*lead, pl.ds(at, 8), slice(None))]
        for k in range(1, REACH + 1):
            total = total + w[REACH + k] * (
                ref[(*lead, pl.ds(at - k, 8), slice(None))]
                + ref[(*lead, pl.ds(at + k, 8), slice(None))]
            )
        return total

    def smooth_rows(it, slot):
        pair = pairs[slot]
        for d in (0, 1):

            def unpack(d=d):
                project_copy(it, pair, slot, d).wait_recv()
                for n in range(2):
                    proj[it, 2 * pair + n, pl.ds(0 if d == 0 else REACH + ROWS, REACH), :] = proj_in[
                        it, d, 2 * pair + n
                    ].astype(F32)

            dt, dm = SIDES[d]
            guarded(there(-dt, -dm), unpack)
        for n in range(2):
            for half in (0, 8):
                sx[pl.ds(pl.multiple_of((2 * pair + n) * ROWS + half, 8), 8), :] = taper(
                    proj, (it, 2 * pair + n), REACH + half
                )

    def column_copy(it, d):
        dt, dm = COLUMN_SIDES[d]
        src, dst = (pk_r.at[it], cl.at[it]) if dm > 0 else (pk_l.at[it], cr.at[it])
        return pltpu.make_async_remote_copy(
            src_ref=src,
            dst_ref=dst.at[:, pl.ds(REACH if dt == 0 else 0 if dt > 0 else REACH + ROWS, ROWS)],
            send_sem=c_send.at[it, d], recv_sem=c_recv.at[it, d],
            device_id=peer(dt, dm), device_id_type=MESH,
        )

    def send_columns(it):
        for part in range(2):
            for half in (0, 8):
                right = jnp.zeros((8, COLS), F32)
                left = jnp.zeros((8, COLS), F32)
                for n in range(8):
                    v = proj[it, 8 * part + n, REACH + half : REACH + half + 8, :]
                    right = jnp.where(group == n, pltpu.roll(v, (16 * n - 112) % COLS, 1), right)
                    left = jnp.where(group == n, pltpu.roll(v, 16 * n, 1), left)
                pk_r[it, part, half : half + 8, :] = right
                pk_l[it, part, half : half + 8, :] = left
        for d, side in enumerate(COLUMN_SIDES):
            guarded(there(*side), column_copy(it, d).start)

    def split(x):
        high = x.astype(BF16)
        return high, (x - high.astype(F32)).astype(BF16)

    def times(x, which):
        high, low = split(x)
        dot = functools.partial(jnp.dot, preferred_element_type=F32)
        return dot(high, band[which, 0]) + (dot(low, band[which, 0]) + dot(high, band[which, 1]))

    def smooth_columns(it):
        z[...] = times(sx[...], 0)
        for d, (dt, dm) in enumerate(COLUMN_SIDES):
            guarded(there(-dt, -dm), column_copy(it, d).wait_recv)
        outer = []
        for which, ref in ((1, cl), (2, cr)):
            x = jnp.concatenate(
                [taper(ref, (it, part), REACH + half) for part in range(2) for half in (0, 8)]
            )
            outer.append(times(x, which))
        for part in range(2):
            for half in (0, 8):
                at = part * ROWS + half
                from_left, from_right = (x[at : at + 8, :] for x in outer)
                for n in range(8):
                    to = (8 * part + n) * ROWS + half
                    z[to : to + 8, :] = z[to : to + 8, :] + jnp.where(
                        lane < 16,
                        pltpu.roll(from_left, (-16 * n) % COLS, 1),
                        jnp.where(
                            lane >= 112, pltpu.roll(from_right, (112 - 16 * n) % COLS, 1), 0.0
                        ),
                    )

    def increments(it):
        width = 4

        def levels(step, carry):
            sums = [jnp.zeros((ROWS, COLS), F32) for _ in range(width)]
            for pair in range(8):
                for n in range(2):
                    v = z[pl.ds((2 * pair + n) * ROWS, ROWS), :]
                    for i in range(width):
                        sums[i] = sums[i] + mt[pair, n, width * step + i].astype(F32) * v
            for i in range(width):
                l = width * step + i
                if it == 0:
                    half = relax * sums[i]
                    out_ref[l] = half
                    v = res[l] - half
                    a1[pl.ds(HALO * LEV + l, 8, stride=LEV), :] = v[0:8]
                    a1[pl.ds((HALO + 8) * LEV + l, 8, stride=LEV), :] = v[8:16]
                else:
                    out_ref[l] = out_ref[l] + relax * sums[i]
            return carry

        for half in range(HALVES):
            first = half * HLEV // width
            lax.fori_loop(first, first + HLEV // width, levels, 0)
            if it == 0:
                send_rows(1, half)

    adjoint(0)
    own_copy.wait()
    project(0, pairs[0], 0, LEV, True)
    send_project(0, 0)
    for i, c in ORDER:
        member_copy(i, c).wait_recv()
        project(0, pairs[1 + i], c * CLEV, CLEV, c == 0)
        if c == CHUNKS - 1:
            send_project(0, 1 + i)
    send_columns(0)
    for slot in range(8):
        smooth_rows(0, slot)
    smooth_columns(0)
    increments(0)

    send_halos(1)
    adjoint(1)
    for slot in range(8):
        project(1, pairs[slot], 0, LEV, True)
        send_project(1, slot)
    send_columns(1)
    for slot in range(8):
        smooth_rows(1, slot)
    smooth_columns(1)
    increments(1)

    for i, c in ORDER:
        member_copy(i, c).wait_send()
    for it in range(2):
        for d in (0, 1):
            for half in range(HALVES):
                guarded(there(*SIDES[d]), row_copy(it, d, half).wait_send)
        for d in range(2, 8):
            guarded(there(*SIDES[d]), quad_copy(it, d).wait_send)
        for slot in range(8):
            for d in (0, 1):
                guarded(there(*SIDES[d]), project_copy(it, pairs[slot], slot, d).wait_send)
        for d, side in enumerate(COLUMN_SIDES):
            guarded(there(*side), column_copy(it, d).wait_send)


def per_device(tiles, blocks, residual_in, members, wind_x, wind_y):
    vmem = pltpu.VMEM
    dma = lambda *shape: pltpu.SemaphoreType.DMA(shape)
    anywhere = pl.BlockSpec(memory_space=pl.ANY)
    extended = vmem((XROWS * LEV, COLS), F32)
    coefficient = vmem((LEV, COLS), F32)
    half = pl.pallas_call(
        functools.partial(kernel, tiles, blocks),
        out_shape=jax.ShapeDtypeStruct((LEV, ROWS, COLS), F32),
        in_specs=[anywhere] * 4,
        out_specs=pl.BlockSpec(memory_space=vmem),
        scratch_shapes=[
            vmem((LEV, ROWS, COLS), F32),
            vmem((8, 2, LEV, ROWS, COLS), BF16),
            extended, extended, extended, extended,
            coefficient, coefficient, coefficient,
            vmem((XROWS, 8, COLS), F32),
            vmem((STEPS, XROWS, 8, COLS), F32),
            vmem((STEPS, XROWS, 8, COLS), F32),
            vmem((2, 4, 8, COLS), F32), vmem((2, 4, 8, COLS), F32),
            vmem((2, 6, 8, COLS), F32), vmem((2, 6, 8, COLS), F32),
            vmem((ROWS * LEV, COLS), F32),
            vmem((LEV, ROWS, COLS), F32),
            vmem((2, 2, HALVES, HALO * HLEV, COLS), BF16),
            vmem((2, 2, HALVES, HALO * HLEV, COLS), BF16),
            vmem((2, 16, ROWS + 2 * REACH, COLS), F32),
            vmem((2, 16, ROWS, COLS), BF16),
            vmem((2, 2, 16, REACH, COLS), BF16),
            vmem((16 * ROWS, COLS), F32),
            vmem((2, 2, ROWS, COLS), F32), vmem((2, 2, ROWS, COLS), F32),
            vmem((2, 2, ROWS + 2 * REACH, COLS), F32),
            vmem((2, 2, ROWS + 2 * REACH, COLS), F32),
            vmem((3, 2, COLS, COLS), BF16),
            vmem((16 * ROWS, COLS), F32),
            pltpu.SMEM((LEV,), F32), pltpu.SMEM((LEV,), F32),
            pltpu.SemaphoreType.DMA, pltpu.SemaphoreType.DMA, dma(2),
            dma(len(FLOWS), CHUNKS), dma(len(FLOWS), CHUNKS),
            dma(2, 8), dma(2, 8),
            dma(2, 2, HALVES), dma(2, 2, HALVES),
            dma(2, 8, 2), dma(2, 8, 2),
            dma(2, len(COLUMN_SIDES)), dma(2, len(COLUMN_SIDES)),
        ],
        compiler_params=pltpu.CompilerParams(collective_id=0, has_side_effects=True),
        name="ensemble_step",
    )(residual_in, members, wind_x, wind_y)
    return (half * (1.0 / relax), residual_in - half)


def solution(mesh):
    return jax.shard_map(
        functools.partial(per_device, mesh.shape["tile"], mesh.shape["member"]),
        mesh=mesh,
        in_specs=(P(None, "tile", "member"), P("member", None, "tile", None), P(), P()),
        out_specs=(P(None, "tile", "member"), P(None, "tile", "member")),
        check_vma=False,
    )
```

```python
import functools

import jax
import jax.numpy as jnp
from jax import lax
from jax.experimental import pallas as pl
from jax.experimental.pallas import tpu as pltpu
from jax.sharding import PartitionSpec as P

MESH = pl.DeviceIdType.MESH
F32 = jnp.float32
BF16 = jnp.bfloat16

LEV = 64
ROWS = 16
COLS = 128
GROUPS = LEV // 8
STEPS = 4
HALO = STEPS
XROWS = ROWS + 2 * HALO
REACH = 16
CHUNKS = 8
CLEV = LEV // CHUNKS

diffusion = 0.1
relax = 0.5

FLOWS = ((2, 1), (0, 1), (2, 0), (1, 1), (3, 1), (1, 0), (3, 0))
ORDER = [(i, c) for c in range(CHUNKS) for i in (0, 1, 2)]
ORDER += [(i, c) for c in range(CHUNKS) for i in (3, 4, 5, 6)]
FIRST = 6
HALVES = 2
HLEV = LEV // HALVES
PARTS = 4
SIDES = ((1, 0), (-1, 0), (0, 1), (0, -1), (1, 1), (-1, 1), (1, -1), (-1, -1))


COLUMN_SIDES = ((1, 1), (-1, 1), (1, -1), (-1, -1), (0, 1), (0, -1))


def taper_weights():
    raw = [1.0 - (k / 17.0) ** 2 for k in range(-16, 17)]
    total = sum(raw)
    return [value / total for value in raw]


def kernel(
    tiles, blocks,
    res_hbm, mem_hbm, wx_hbm, wy_hbm,
    out_hbm,
    res, mt, a0, a1, w1, w2, w3, c0, ax, ay, own, strip, sides, powers, mr, ml, ql, qr, gt, g,
    row_out, row_in, proj, proj_out, proj_in, sx, pk_r, pk_l, cl, cr, band, z, half_ref,
    wx_ref, wy_ref, own_sem, res_sem, wind_sem, out_sem, m_send, m_recv, h_send, h_recv, r_send, r_recv, p_send, p_recv, c_send, c_recv,
):
    t = lax.axis_index("tile")
    m = lax.axis_index("member")
    zh, y = m // 4, m % 4
    w = taper_weights()

    def there(dt, dm):
        ok = None
        for cond in ([t < tiles - 1] if dt > 0 else [t > 0] if dt < 0 else []) + (
            [m < blocks - 1] if dm > 0 else [m > 0] if dm < 0 else []
        ):
            ok = cond if ok is None else jnp.logical_and(ok, cond)
        return ok

    def peer(dt, dm):
        return ((t + dt + tiles) % tiles, (m + dm + blocks) % blocks)

    def mate(dy, dz):
        return ((zh + dz) % 2) * 4 + (y + dy + 4) % 4

    res_copy = pltpu.make_async_copy(res_hbm, res, res_sem)
    res_copy.start()
    wind_copies = [
        pltpu.make_async_copy(wind, wind_ref, wind_sem.at[n])
        for n, (wind, wind_ref) in enumerate(((wx_hbm, wx_ref), (wy_hbm, wy_ref)))
    ]
    for copy in wind_copies:
        copy.start()
    own_copy = pltpu.make_async_copy(
        mem_hbm.at[:, :, :, pl.ds(pl.multiple_of(m * COLS, COLS), COLS)], mt.at[m], own_sem
    )
    own_copy.start()

    barrier = pltpu.get_barrier_semaphore()
    count = jnp.int32(len(FLOWS))
    for dy, dz in FLOWS:
        pl.semaphore_signal(barrier, inc=1, device_id=(t, mate(dy, dz)), device_id_type=MESH)
    for dt, dm in SIDES:
        if dt == 0:
            continue
        ok = there(dt, dm)
        count = count + ok.astype(jnp.int32)

        @pl.when(ok)
        def _():
            pl.semaphore_signal(barrier, inc=1, device_id=peer(dt, dm), device_id_type=MESH)

    pl.semaphore_wait(barrier, count)

    def member_copy(i, c):
        dy, dz = FLOWS[i]
        target = mate(dy, dz)
        return pltpu.make_async_remote_copy(
            src_ref=mem_hbm.at[
                :, pl.ds(c * CLEV, CLEV), :, pl.ds(pl.multiple_of(target * COLS, COLS), COLS)
            ],
            dst_ref=mt.at[m, :, pl.ds(c * CLEV, CLEV)],
            send_sem=m_send.at[i, c],
            recv_sem=m_recv.at[i, c],
            device_id=(t, target),
            device_id_type=MESH,
        )

    for i, c in ORDER[:FIRST]:
        member_copy(i, c).start()

    @pl.when(t == 0)
    def _():
        for a in (a0, a1):
            a[pl.ds(0, HALO * LEV), :] = jnp.zeros((HALO * LEV, COLS), F32)
        own[:, 0:HALO] = jnp.zeros((2, HALO, 8, COLS), F32)
        ql[:, 0] = jnp.zeros((2, 8, COLS), F32)
        qr[:, 0] = jnp.zeros((2, 8, COLS), F32)
        proj[:, :, 0:REACH, :] = jnp.zeros((2, 16, REACH, COLS), F32)
        cl[:, :, 0:REACH, :] = jnp.zeros((2, 2, REACH, COLS), F32)
        cr[:, :, 0:REACH, :] = jnp.zeros((2, 2, REACH, COLS), F32)

    @pl.when(t == tiles - 1)
    def _():
        for a in (a0, a1):
            a[pl.ds((HALO + ROWS) * LEV, HALO * LEV), :] = jnp.zeros((HALO * LEV, COLS), F32)
        own[:, HALO + ROWS :] = jnp.zeros((2, HALO, 8, COLS), F32)
        ql[:, 5] = jnp.zeros((2, 8, COLS), F32)
        qr[:, 5] = jnp.zeros((2, 8, COLS), F32)
        proj[:, :, REACH + ROWS :, :] = jnp.zeros((2, 16, REACH, COLS), F32)
        cl[:, :, REACH + ROWS :, :] = jnp.zeros((2, 2, REACH, COLS), F32)
        cr[:, :, REACH + ROWS :, :] = jnp.zeros((2, 2, REACH, COLS), F32)

    @pl.when(m == 0)
    def _():
        ql[...] = jnp.zeros(ql.shape, F32)
        cl[...] = jnp.zeros(cl.shape, F32)

    @pl.when(m == blocks - 1)
    def _():
        qr[...] = jnp.zeros(qr.shape, F32)
        cr[...] = jnp.zeros(cr.shape, F32)

    lane = lax.broadcasted_iota(jnp.int32, (8, COLS), 1)
    q = lane % 16
    group = lane // 16

    def row_copy(it, d, half):
        return pltpu.make_async_remote_copy(
            src_ref=row_out.at[it, d, half], dst_ref=row_in.at[it, d, half],
            send_sem=r_send.at[it, d, half], recv_sem=r_recv.at[it, d, half],
            device_id=peer(*SIDES[d]), device_id_type=MESH,
        )

    def send_rows(it, half):
        a = (a0, a1)[it]
        for d, first in ((0, ROWS), (1, HALO)):
            for r in range(HALO):
                row_out[it, d, half, r * HLEV : (r + 1) * HLEV, :] = a[
                    (first + r) * LEV + half * HLEV : (first + r) * LEV + (half + 1) * HLEV, :
                ].astype(BF16)
            guarded(there(*SIDES[d]), row_copy(it, d, half).start)

    def receive_rows(it):
        a = (a0, a1)[it]
        for d, first in ((0, 0), (1, HALO + ROWS)):

            def unpack(d=d, first=first):
                for half in range(HALVES):
                    row_copy(it, d, half).wait_recv()
                    for r in range(HALO):
                        at = (first + r) * LEV + half * HLEV
                        a[at : at + HLEV, :] = row_in[
                            it, d, half, r * HLEV : (r + 1) * HLEV, :
                        ].astype(F32)

            dt, dm = SIDES[d]
            guarded(there(-dt, -dm), unpack)

    def quad_copy(it, d):
        dt, dm = SIDES[d]
        src, dst = (mr.at[it], ql.at[it]) if dm > 0 else (ml.at[it], qr.at[it])
        if dm == 0:
            src = own.at[it, pl.ds(ROWS if dt > 0 else HALO, HALO)]
            dst = own.at[it, pl.ds(0 if dt > 0 else HALO + ROWS, HALO)]
        elif dt == 0:
            src, dst = src, dst.at[pl.ds(1, 4)]
        elif dt > 0:
            src, dst = src.at[pl.ds(3, 1)], dst.at[pl.ds(0, 1)]
        else:
            src, dst = src.at[pl.ds(0, 1)], dst.at[pl.ds(5, 1)]
        return pltpu.make_async_remote_copy(
            src_ref=src, dst_ref=dst, send_sem=h_send.at[it, d], recv_sem=h_recv.at[it, d],
            device_id=peer(dt, dm), device_id_type=MESH,
        )

    def guarded(ok, action):
        if ok is None:
            action()
        else:
            pl.when(ok)(action)

    def edges(a, r):
        total = jnp.zeros((8, COLS), F32)
        for k in range(GROUPS):
            v = a[pl.ds(pl.multiple_of(r * LEV + 8 * k, 8), 8), :]
            low = pltpu.roll(v, (16 * k + 4) % COLS, 1)
            high = pltpu.roll(v, (16 * k + 12) % COLS, 1)
            part = jnp.where(q < 8, low, high)
            total = jnp.where(group == k, part, total)
        return total

    def send_halos(it):
        a = (a0, a1)[it]

        def pack(r, carry):
            own[it, HALO + r] = edges(a, HALO + r)
            return carry

        def pack_ends(r, carry):
            return pack(r + ROWS - HALO, pack(r, carry))

        def quads(numbers):
            for quad in numbers:
                right = jnp.zeros((8, COLS), F32)
                left = jnp.zeros((8, COLS), F32)
                for k in range(4):
                    v = own[it, HALO + 4 * quad + k]
                    here = q // 4 == k
                    right = jnp.where(here, pltpu.roll(v, (4 * k - 8) % COLS, 1), right)
                    left = jnp.where(here, pltpu.roll(v, (4 * k - 4) % COLS, 1), left)
                mr[it, quad] = right
                ml[it, quad] = left

        lax.fori_loop(0, HALO, pack_ends, 0, unroll=HALO if it else 1)
        quads((0, 3))
        for d in (4, 5, 6, 7, 0, 1):
            guarded(there(*SIDES[d]), quad_copy(it, d).start)
        lax.fori_loop(HALO, ROWS - HALO, pack, 0, unroll=ROWS - 2 * HALO if it else 1)
        quads((1, 2))
        for d in (2, 3):
            guarded(there(*SIDES[d]), quad_copy(it, d).start)

    res_copy.wait()

    def spread(l, carry):
        v = res[l]
        a0[pl.ds(HALO * LEV + l, 8, stride=LEV), :] = v[0:8]
        a0[pl.ds((HALO + 8) * LEV + l, 8, stride=LEV), :] = v[8:16]
        return carry

    lax.fori_loop(0, LEV, spread, 0, unroll=4)
    for half in range(HALVES):
        send_rows(0, half)
    send_halos(0)
    for i, c in ORDER[FIRST:]:
        member_copy(i, c).start()

    for copy in wind_copies:
        copy.wait()

    def coefficients(l, carry):
        wx, wy = wx_ref[l], wy_ref[l]
        c0[pl.ds(l, 1), :] = jnp.full((1, COLS), (1.0 - 4.0 * diffusion - wx - wy) / diffusion, F32)
        ax[pl.ds(l, 1), :] = jnp.full((1, COLS), (diffusion + wx) / diffusion, F32)
        ay[pl.ds(l, 1), :] = jnp.full((1, COLS), (diffusion + wy) / diffusion, F32)
        return carry

    lax.fori_loop(0, LEV, coefficients, 0)

    total_w = sum(1.0 - (i / 17.0) ** 2 for i in range(-16, 17))
    source = lax.broadcasted_iota(jnp.int32, (COLS, COLS), 0)
    target = lax.broadcasted_iota(jnp.int32, (COLS, COLS), 1)
    together = source // 16 == target // 16
    for which, k, near in (
        (0, source - target, None),
        (1, source - 16 - target, together),
        (2, source + 16 - target, together),
    ):
        kf = k.astype(F32)
        reached = jnp.abs(k) <= REACH
        if near is not None:
            reached = jnp.logical_and(reached, near)
        full = jnp.where(reached, (1.0 - kf * kf * (1.0 / 289.0)) * (1.0 / total_w), 0.0)
        coarse = full.astype(BF16)
        band[which, 0] = coarse
        band[which, 1] = (full - coarse.astype(F32)).astype(BF16)

    def strip_coefficient(ref):
        total = jnp.zeros((8, COLS), F32)
        for k in range(GROUPS):
            total = jnp.where(group == k, ref[8 * k : 8 * k + 8, :], total)
        return total

    row_low = jnp.where(t > 0, 1.0, 0.0).astype(F32)
    row_high = jnp.where(t < tiles - 1, 1.0, 0.0).astype(F32)
    inside = jnp.logical_and(
        jnp.logical_or(q >= 4, m > 0), jnp.logical_or(q < 12, m < blocks - 1)
    )
    strip_mask = jnp.where(inside, 1.0, 0.0).astype(F32)

    binomial = (1.0, 4.0, 6.0, 4.0, 1.0)

    def column_powers(a, r, most):
        for k in range(GROUPS):
            here = pl.ds(pl.multiple_of(r * LEV + 8 * k, 8), 8)
            x = a[here, :]
            for power in range(1, most + 1):
                left = jnp.where(lane == 0, 0.0, pltpu.roll(x, 1, 1))
                right = jnp.where(lane == COLS - 1, 0.0, pltpu.roll(x, COLS - 1, 1))
                x = left + ay[8 * k : 8 * k + 8, :] * right
                powers[power - 1, here, :] = x

    def adjoint_early(it):
        def row(r, carry):
            column_powers((a0, a1)[it], r, STEPS)
            return carry

        lax.fori_loop(HALO, HALO + ROWS, row, 0, unroll=4 if it else 1)
        for stage in range(1, STEPS + 1):
            lax.fori_loop(
                HALO + stage, HALO + ROWS - stage, functools.partial(row_stage, it, stage), 0,
                unroll=2 if it else 1,
            )

    def row_stage(it, stage, r, carry, scale=None):
        src = ((a0, a1)[it], w1, w2, w3)[stage - 1]
        dst = (w1, w2, w3, gt)[stage - 1]
        for k in range(GROUPS):
            at = r * LEV + 8 * k
            here = pl.ds(pl.multiple_of(at, 8), 8)
            s = slice(8 * k, 8 * k + 8)
            out = (
                c0[s, :] * src[here, :]
                + src[pl.ds(pl.multiple_of(at - LEV, 8), 8), :]
                + ax[s, :] * src[pl.ds(pl.multiple_of(at + LEV, 8), 8), :]
            )
            side = powers[stage - 1, here, :]
            out = out + (side if stage == STEPS else binomial[stage] * side)
            if scale is not None:
                out = out * scale
            if stage == STEPS:
                dst[pl.ds(pl.multiple_of(at - HALO * LEV, 8), 8), :] = out
            else:
                dst[here, :] = out
        return carry

    def adjoint_late(it):
        a = (a0, a1)[it]
        receive_rows(it)
        for r in range(1, HALO):
            column_powers(a, r, r)
            column_powers(a, XROWS - 1 - r, r)
        for stage in range(1, STEPS + 1):
            for r in range(stage, HALO + stage):
                row_stage(it, stage, r, 0, row_low if r < HALO else None)
                r = XROWS - 1 - r
                row_stage(it, stage, r, 0, row_high if r >= HALO + ROWS else None)

        for d in range(8):
            dt, dm = SIDES[d]
            guarded(there(-dt, -dm), quad_copy(it, d).wait_recv)
        for r in range(XROWS):
            left = pltpu.roll(ql[it, r // 4], (-4 * (r % 4)) % COLS, 1)
            right = pltpu.roll(qr[it, r // 4], (12 - 4 * (r % 4)) % COLS, 1)
            strip[0, r] = jnp.where(q < 4, left, jnp.where(q >= 12, right, own[it, r]))
        sc0, sax, say = strip_coefficient(c0), strip_coefficient(ax), strip_coefficient(ay)
        mine = jnp.logical_and(q >= 4, q < 12)

        def strip_step(load, r):
            v = load(r)
            out = (
                sc0 * v
                + (load(r - 1) + pltpu.roll(v, 1, 1))
                + sax * load(r + 1)
                + say * pltpu.roll(v, COLS - 1, 1)
            )
            return out * row_low if r < HALO else out * row_high if r >= HALO + ROWS else out

        for step in range(1, STEPS + 1):

            def joined(r):
                outer = strip[step - 1, r]
                return jnp.where(mine, 0.0 if step == 1 else sides[step - 2, r], outer)

            for r in range(step, XROWS - step):
                sides[step - 1, r] = strip_step(joined, r)
                if step < STEPS:
                    strip[step, r] = strip_step(lambda i: strip[step - 1, i], r) * strip_mask

        def finish(r, carry):
            v = sides[STEPS - 1, HALO + r]
            v = jnp.where(q < 4, pltpu.roll(v, COLS - 8, 1), v)
            for k in range(GROUPS):
                here = pl.ds(pl.multiple_of(r * LEV + 8 * k, 8), 8)
                ends = jnp.where(
                    jnp.logical_or(lane < HALO, lane >= COLS - HALO),
                    pltpu.roll(v, COLS - HALO - 16 * k, 1),
                    0.0,
                )
                out = (gt[here, :] + ends) * diffusion**STEPS
                g[pl.ds(8 * k * ROWS + r, 8, stride=ROWS), :] = out.astype(BF16).astype(F32)
            return carry

        lax.fori_loop(0, ROWS, finish, 0, unroll=4 if it else 1)

    own_rows = pl.ds(REACH, ROWS)

    def project(it, pair, first, count, fresh):
        if fresh:
            start = (jnp.zeros((ROWS, COLS), F32), jnp.zeros((ROWS, COLS), F32))
        else:
            start = (proj[it, 2 * pair, own_rows, :], proj[it, 2 * pair + 1, own_rows, :])

        def level(l, sums):
            v = g[pl.ds(pl.multiple_of(l * ROWS, ROWS), ROWS), :]
            return tuple(s + mt[pair, n, l].astype(F32) * v for n, s in enumerate(sums))

        sums = lax.fori_loop(first, first + count, level, start, unroll=8)
        for n in range(2):
            proj[it, 2 * pair + n, own_rows, :] = sums[n]

    def project_copy(it, pair, slot, d):
        return pltpu.make_async_remote_copy(
            src_ref=proj_out.at[it, pl.ds(2 * pair, 2)],
            dst_ref=proj_in.at[it, d, pl.ds(2 * pair, 2)],
            send_sem=p_send.at[it, slot, d], recv_sem=p_recv.at[it, slot, d],
            device_id=peer(*SIDES[d]), device_id_type=MESH,
        )

    pairs = [m] + [mate(-dy, dz) for dy, dz in FLOWS]

    def send_project(it, slot):
        for n in range(2):
            member = 2 * pairs[slot] + n
            proj_out[it, member] = proj[it, member, own_rows, :].astype(BF16)
        for d in (0, 1):
            guarded(there(*SIDES[d]), project_copy(it, pairs[slot], slot, d).start)

    def taper(ref, lead, at):
        total = w[REACH] * ref[(*lead, pl.ds(at, 8), slice(None))]
        for k in range(1, REACH + 1):
            total = total + w[REACH + k] * (
                ref[(*lead, pl.ds(at - k, 8), slice(None))]
                + ref[(*lead, pl.ds(at + k, 8), slice(None))]
            )
        return total

    def smooth_rows(it, slot):
        pair = pairs[slot]
        for d in (0, 1):

            def unpack(d=d):
                project_copy(it, pair, slot, d).wait_recv()
                for n in range(2):
                    proj[it, 2 * pair + n, pl.ds(0 if d == 0 else REACH + ROWS, REACH), :] = proj_in[
                        it, d, 2 * pair + n
                    ].astype(F32)

            dt, dm = SIDES[d]
            guarded(there(-dt, -dm), unpack)
        for n in range(2):
            for half in (0, 8):
                sx[pl.ds(pl.multiple_of((2 * pair + n) * ROWS + half, 8), 8), :] = taper(
                    proj, (it, 2 * pair + n), REACH + half
                )

    def column_copy(it, d):
        dt, dm = COLUMN_SIDES[d]
        src, dst = (pk_r.at[it], cl.at[it]) if dm > 0 else (pk_l.at[it], cr.at[it])
        return pltpu.make_async_remote_copy(
            src_ref=src,
            dst_ref=dst.at[:, pl.ds(REACH if dt == 0 else 0 if dt > 0 else REACH + ROWS, ROWS)],
            send_sem=c_send.at[it, d], recv_sem=c_recv.at[it, d],
            device_id=peer(dt, dm), device_id_type=MESH,
        )

    def send_columns(it):
        for part in range(2):
            for half in (0, 8):
                right = jnp.zeros((8, COLS), F32)
                left = jnp.zeros((8, COLS), F32)
                for n in range(8):
                    v = proj[it, 8 * part + n, REACH + half : REACH + half + 8, :]
                    right = jnp.where(group == n, pltpu.roll(v, (16 * n - 112) % COLS, 1), right)
                    left = jnp.where(group == n, pltpu.roll(v, 16 * n, 1), left)
                pk_r[it, part, half : half + 8, :] = right
                pk_l[it, part, half : half + 8, :] = left
        for d, side in enumerate(COLUMN_SIDES):
            guarded(there(*side), column_copy(it, d).start)

    def split(x):
        high = x.astype(BF16)
        return high, (x - high.astype(F32)).astype(BF16)

    def times(x, which):
        high, low = split(x)
        dot = functools.partial(jnp.dot, preferred_element_type=F32)
        return dot(high, band[which, 0]) + (dot(low, band[which, 0]) + dot(high, band[which, 1]))

    def smooth_columns(it):
        z[...] = times(sx[...], 0)
        for d, (dt, dm) in enumerate(COLUMN_SIDES):
            guarded(there(-dt, -dm), column_copy(it, d).wait_recv)
        outer = []
        for which, ref in ((1, cl), (2, cr)):
            x = jnp.concatenate(
                [taper(ref, (it, part), REACH + half) for part in range(2) for half in (0, 8)]
            )
            outer.append(times(x, which))
        for part in range(2):
            for half in (0, 8):
                at = part * ROWS + half
                from_left, from_right = (x[at : at + 8, :] for x in outer)
                for n in range(8):
                    to = (8 * part + n) * ROWS + half
                    z[to : to + 8, :] = z[to : to + 8, :] + jnp.where(
                        lane < 16,
                        pltpu.roll(from_left, (-16 * n) % COLS, 1),
                        jnp.where(
                            lane >= 112, pltpu.roll(from_right, (112 - 16 * n) % COLS, 1), 0.0
                        ),
                    )

    def out_copy(part):
        levels = pl.ds(part * (LEV // PARTS), LEV // PARTS)
        return pltpu.make_async_copy(half_ref.at[levels], out_hbm.at[levels], out_sem.at[part])

    def increments(it):
        width = 4

        def levels(step, carry):
            sums = [jnp.zeros((ROWS, COLS), F32) for _ in range(width)]
            for pair in range(8):
                for n in range(2):
                    v = z[pl.ds((2 * pair + n) * ROWS, ROWS), :]
                    for i in range(width):
                        sums[i] = sums[i] + mt[pair, n, width * step + i].astype(F32) * v
            for i in range(width):
                l = width * step + i
                if it == 0:
                    half = relax * sums[i]
                    half_ref[l] = half
                    v = res[l] - half
                    a1[pl.ds(HALO * LEV + l, 8, stride=LEV), :] = v[0:8]
                    a1[pl.ds((HALO + 8) * LEV + l, 8, stride=LEV), :] = v[8:16]
                else:
                    half_ref[l] = half_ref[l] + relax * sums[i]
            return carry

        parts = PARTS if it else HALVES
        for part in range(parts):
            count = LEV // parts // width
            lax.fori_loop(part * count, (part + 1) * count, levels, 0)
            if it == 0:
                send_rows(1, part)
            else:
                out_copy(part).start()

    def halos_sent(it):
        for d in (0, 1):
            for half in range(HALVES):
                guarded(there(*SIDES[d]), row_copy(it, d, half).wait_send)
        for d in range(8):
            guarded(there(*SIDES[d]), quad_copy(it, d).wait_send)

    def projects_sent(it):
        for slot in range(8):
            for d in (0, 1):
                guarded(there(*SIDES[d]), project_copy(it, pairs[slot], slot, d).wait_send)

    def columns_sent(it):
        for d, side in enumerate(COLUMN_SIDES):
            guarded(there(*side), column_copy(it, d).wait_send)

    adjoint_early(0)
    adjoint_late(0)
    own_copy.wait()
    project(0, pairs[0], 0, LEV, True)
    send_project(0, 0)
    for i, c in ORDER:
        member_copy(i, c).wait_recv()
        project(0, pairs[1 + i], c * CLEV, CLEV, c == 0)
        if c == CHUNKS - 1:
            send_project(0, 1 + i)
    send_columns(0)
    for slot in range(8):
        smooth_rows(0, slot)
    smooth_columns(0)
    increments(0)

    send_halos(1)
    adjoint_early(1)
    for i, c in ORDER:
        member_copy(i, c).wait_send()
    halos_sent(0)
    projects_sent(0)
    columns_sent(0)
    adjoint_late(1)
    for slot in range(8):
        project(1, pairs[slot], 0, LEV, True)
        send_project(1, slot)
    send_columns(1)
    halos_sent(1)
    for slot in range(8):
        smooth_rows(1, slot)
    projects_sent(1)
    smooth_columns(1)
    increments(1)
    columns_sent(1)
    for part in range(PARTS):
        out_copy(part).wait()


def per_device(tiles, blocks, residual_in, members, wind_x, wind_y):
    vmem = pltpu.VMEM
    dma = lambda *shape: pltpu.SemaphoreType.DMA(shape)
    anywhere = pl.BlockSpec(memory_space=pl.ANY)
    extended = vmem((XROWS * LEV, COLS), F32)
    coefficient = vmem((LEV, COLS), F32)
    half = pl.pallas_call(
        functools.partial(kernel, tiles, blocks),
        out_shape=jax.ShapeDtypeStruct((LEV, ROWS, COLS), F32),
        in_specs=[anywhere] * 4,
        out_specs=anywhere,
        scratch_shapes=[
            vmem((LEV, ROWS, COLS), F32),
            vmem((8, 2, LEV, ROWS, COLS), BF16),
            extended, extended, extended, extended, extended,
            coefficient, coefficient, coefficient,
            vmem((2, XROWS, 8, COLS), F32),
            vmem((STEPS, XROWS, 8, COLS), F32),
            vmem((STEPS, XROWS, 8, COLS), F32),
            vmem((STEPS, XROWS * LEV, COLS), F32),
            vmem((2, 4, 8, COLS), F32), vmem((2, 4, 8, COLS), F32),
            vmem((2, 6, 8, COLS), F32), vmem((2, 6, 8, COLS), F32),
            vmem((ROWS * LEV, COLS), F32),
            vmem((LEV * ROWS, COLS), F32),
            vmem((2, 2, HALVES, HALO * HLEV, COLS), BF16),
            vmem((2, 2, HALVES, HALO * HLEV, COLS), BF16),
            vmem((2, 16, ROWS + 2 * REACH, COLS), F32),
            vmem((2, 16, ROWS, COLS), BF16),
            vmem((2, 2, 16, REACH, COLS), BF16),
            vmem((16 * ROWS, COLS), F32),
            vmem((2, 2, ROWS, COLS), F32), vmem((2, 2, ROWS, COLS), F32),
            vmem((2, 2, ROWS + 2 * REACH, COLS), F32),
            vmem((2, 2, ROWS + 2 * REACH, COLS), F32),
            vmem((3, 2, COLS, COLS), BF16),
            vmem((16 * ROWS, COLS), F32),
            vmem((LEV, ROWS, COLS), F32),
            pltpu.SMEM((LEV,), F32), pltpu.SMEM((LEV,), F32),
            pltpu.SemaphoreType.DMA, pltpu.SemaphoreType.DMA, dma(2), dma(PARTS),
            dma(len(FLOWS), CHUNKS), dma(len(FLOWS), CHUNKS),
            dma(2, 8), dma(2, 8),
            dma(2, 2, HALVES), dma(2, 2, HALVES),
            dma(2, 8, 2), dma(2, 8, 2),
            dma(2, len(COLUMN_SIDES)), dma(2, len(COLUMN_SIDES)),
        ],
        compiler_params=pltpu.CompilerParams(collective_id=0, has_side_effects=True),
        name="ensemble_step",
    )(residual_in, members, wind_x, wind_y)
    return (half * (1.0 / relax), residual_in - half)


def solution(mesh):
    return jax.shard_map(
        functools.partial(per_device, mesh.shape["tile"], mesh.shape["member"]),
        mesh=mesh,
        in_specs=(P(None, "tile", "member"), P("member", None, "tile", None), P(), P()),
        out_specs=(P(None, "tile", "member"), P(None, "tile", "member")),
        check_vma=False,
    )
```

```python
import functools

import jax
import jax.numpy as jnp
from jax import lax
from jax.experimental import pallas as pl
from jax.experimental.pallas import tpu as pltpu
from jax.sharding import PartitionSpec as P

MESH = pl.DeviceIdType.MESH
F32 = jnp.float32
BF16 = jnp.bfloat16

LEV = 64
ROWS = 16
COLS = 128
GROUPS = LEV // 8
STEPS = 4
HALO = STEPS
XROWS = ROWS + 2 * HALO
REACH = 16
CHUNKS = 8
CLEV = LEV // CHUNKS

diffusion = 0.1
relax = 0.5

FLOWS = ((2, 1), (0, 1), (2, 0), (1, 1), (3, 1), (1, 0), (3, 0))
ORDER = [(i, c) for c in range(CHUNKS) for i in (0, 1, 2)]
ORDER += [(i, c) for c in range(CHUNKS) for i in (3, 4, 5, 6)]
FIRST = 6
HALVES = 2
HLEV = LEV // HALVES
PARTS = 4
SIDES = ((1, 0), (-1, 0), (0, 1), (0, -1), (1, 1), (-1, 1), (1, -1), (-1, -1))


COLUMN_SIDES = ((1, 1), (-1, 1), (1, -1), (-1, -1), (0, 1), (0, -1))


def taper_weights():
    raw = [1.0 - (k / 17.0) ** 2 for k in range(-16, 17)]
    total = sum(raw)
    return [value / total for value in raw]


def kernel(
    tiles, blocks,
    res_hbm, mem_hbm, wx_hbm, wy_hbm,
    out_hbm,
    res, mt, a0, a1, w1, w2, w3, c0, ax, ay, own, strip, sides, powers, mr, ml, ql, qr, gt, g,
    row_out, row_in, proj, proj_out, proj_in, sx, pk_r, pk_l, cl_in, cr_in, cl, cr, band, z, half_ref,
    wx_ref, wy_ref, own_sem, res_sem, wind_sem, out_sem, m_send, m_recv, h_send, h_recv, r_send, r_recv, p_send, p_recv, c_send, c_recv,
):
    t = lax.axis_index("tile")
    m = lax.axis_index("member")
    zh, y = m // 4, m % 4
    w = taper_weights()

    def there(dt, dm):
        ok = None
        for cond in ([t < tiles - 1] if dt > 0 else [t > 0] if dt < 0 else []) + (
            [m < blocks - 1] if dm > 0 else [m > 0] if dm < 0 else []
        ):
            ok = cond if ok is None else jnp.logical_and(ok, cond)
        return ok

    def peer(dt, dm):
        return ((t + dt + tiles) % tiles, (m + dm + blocks) % blocks)

    def mate(dy, dz):
        return ((zh + dz) % 2) * 4 + (y + dy + 4) % 4

    res_copy = pltpu.make_async_copy(res_hbm, res, res_sem)
    res_copy.start()
    wind_copies = [
        pltpu.make_async_copy(wind, wind_ref, wind_sem.at[n])
        for n, (wind, wind_ref) in enumerate(((wx_hbm, wx_ref), (wy_hbm, wy_ref)))
    ]
    for copy in wind_copies:
        copy.start()
    own_copy = pltpu.make_async_copy(
        mem_hbm.at[:, :, :, pl.ds(pl.multiple_of(m * COLS, COLS), COLS)], mt.at[m], own_sem
    )
    own_copy.start()

    barrier = pltpu.get_barrier_semaphore()
    count = jnp.int32(len(FLOWS))
    for dy, dz in FLOWS:
        pl.semaphore_signal(barrier, inc=1, device_id=(t, mate(dy, dz)), device_id_type=MESH)
    for dt, dm in SIDES:
        if dt == 0:
            continue
        ok = there(dt, dm)
        count = count + ok.astype(jnp.int32)

        @pl.when(ok)
        def _():
            pl.semaphore_signal(barrier, inc=1, device_id=peer(dt, dm), device_id_type=MESH)

    pl.semaphore_wait(barrier, count)

    def member_copy(i, c):
        dy, dz = FLOWS[i]
        target = mate(dy, dz)
        return pltpu.make_async_remote_copy(
            src_ref=mem_hbm.at[
                :, pl.ds(c * CLEV, CLEV), :, pl.ds(pl.multiple_of(target * COLS, COLS), COLS)
            ],
            dst_ref=mt.at[m, :, pl.ds(c * CLEV, CLEV)],
            send_sem=m_send.at[i, c],
            recv_sem=m_recv.at[i, c],
            device_id=(t, target),
            device_id_type=MESH,
        )

    for i, c in ORDER[:FIRST]:
        member_copy(i, c).start()

    @pl.when(t == 0)
    def _():
        for a in (a0, a1):
            a[pl.ds(0, HALO * LEV), :] = jnp.zeros((HALO * LEV, COLS), F32)
        own[:, 0:HALO] = jnp.zeros((2, HALO, 8, COLS), F32)
        ql[:, 0] = jnp.zeros((2, 8, COLS), F32)
        qr[:, 0] = jnp.zeros((2, 8, COLS), F32)
        proj[:, :, 0:REACH, :] = jnp.zeros((2, 16, REACH, COLS), F32)
        cl[:, :, 0:REACH, :] = jnp.zeros((2, 2, REACH, COLS), F32)
        cr[:, :, 0:REACH, :] = jnp.zeros((2, 2, REACH, COLS), F32)

    @pl.when(t == tiles - 1)
    def _():
        for a in (a0, a1):
            a[pl.ds((HALO + ROWS) * LEV, HALO * LEV), :] = jnp.zeros((HALO * LEV, COLS), F32)
        own[:, HALO + ROWS :] = jnp.zeros((2, HALO, 8, COLS), F32)
        ql[:, 5] = jnp.zeros((2, 8, COLS), F32)
        qr[:, 5] = jnp.zeros((2, 8, COLS), F32)
        proj[:, :, REACH + ROWS :, :] = jnp.zeros((2, 16, REACH, COLS), F32)
        cl[:, :, REACH + ROWS :, :] = jnp.zeros((2, 2, REACH, COLS), F32)
        cr[:, :, REACH + ROWS :, :] = jnp.zeros((2, 2, REACH, COLS), F32)

    @pl.when(m == 0)
    def _():
        ql[...] = jnp.zeros(ql.shape, F32)
        cl[...] = jnp.zeros(cl.shape, F32)

    @pl.when(m == blocks - 1)
    def _():
        qr[...] = jnp.zeros(qr.shape, F32)
        cr[...] = jnp.zeros(cr.shape, F32)

    lane = lax.broadcasted_iota(jnp.int32, (8, COLS), 1)
    q = lane % 16
    group = lane // 16

    def row_copy(it, d, half):
        return pltpu.make_async_remote_copy(
            src_ref=row_out.at[it, d, half], dst_ref=row_in.at[it, d, half],
            send_sem=r_send.at[it, d, half], recv_sem=r_recv.at[it, d, half],
            device_id=peer(*SIDES[d]), device_id_type=MESH,
        )

    def send_rows(it, half):
        a = (a0, a1)[it]
        for d, first in ((0, ROWS), (1, HALO)):
            for r in range(HALO):
                row_out[it, d, half, r * HLEV : (r + 1) * HLEV, :] = a[
                    (first + r) * LEV + half * HLEV : (first + r) * LEV + (half + 1) * HLEV, :
                ].astype(BF16)
            guarded(there(*SIDES[d]), row_copy(it, d, half).start)

    def receive_rows(it):
        a = (a0, a1)[it]
        for d, first in ((0, 0), (1, HALO + ROWS)):

            def unpack(d=d, first=first):
                for half in range(HALVES):
                    row_copy(it, d, half).wait_recv()
                    for r in range(HALO):
                        at = (first + r) * LEV + half * HLEV
                        a[at : at + HLEV, :] = row_in[
                            it, d, half, r * HLEV : (r + 1) * HLEV, :
                        ].astype(F32)

            dt, dm = SIDES[d]
            guarded(there(-dt, -dm), unpack)

    def quad_copy(it, d):
        dt, dm = SIDES[d]
        src, dst = (mr.at[it], ql.at[it]) if dm > 0 else (ml.at[it], qr.at[it])
        if dm == 0:
            src = own.at[it, pl.ds(ROWS if dt > 0 else HALO, HALO)]
            dst = own.at[it, pl.ds(0 if dt > 0 else HALO + ROWS, HALO)]
        elif dt == 0:
            src, dst = src, dst.at[pl.ds(1, 4)]
        elif dt > 0:
            src, dst = src.at[pl.ds(3, 1)], dst.at[pl.ds(0, 1)]
        else:
            src, dst = src.at[pl.ds(0, 1)], dst.at[pl.ds(5, 1)]
        return pltpu.make_async_remote_copy(
            src_ref=src, dst_ref=dst, send_sem=h_send.at[it, d], recv_sem=h_recv.at[it, d],
            device_id=peer(dt, dm), device_id_type=MESH,
        )

    def guarded(ok, action):
        if ok is None:
            action()
        else:
            pl.when(ok)(action)

    def edges(a, r):
        total = jnp.zeros((8, COLS), F32)
        for k in range(GROUPS):
            v = a[pl.ds(pl.multiple_of(r * LEV + 8 * k, 8), 8), :]
            low = pltpu.roll(v, (16 * k + 4) % COLS, 1)
            high = pltpu.roll(v, (16 * k + 12) % COLS, 1)
            part = jnp.where(q < 8, low, high)
            total = jnp.where(group == k, part, total)
        return total

    def send_halos(it):
        a = (a0, a1)[it]

        def pack(r, carry):
            own[it, HALO + r] = edges(a, HALO + r)
            return carry

        def pack_ends(r, carry):
            return pack(r + ROWS - HALO, pack(r, carry))

        def quads(numbers):
            for quad in numbers:
                right = jnp.zeros((8, COLS), F32)
                left = jnp.zeros((8, COLS), F32)
                for k in range(4):
                    v = own[it, HALO + 4 * quad + k]
                    here = q // 4 == k
                    right = jnp.where(here, pltpu.roll(v, (4 * k - 8) % COLS, 1), right)
                    left = jnp.where(here, pltpu.roll(v, (4 * k - 4) % COLS, 1), left)
                mr[it, quad] = right
                ml[it, quad] = left

        lax.fori_loop(0, HALO, pack_ends, 0, unroll=HALO if it else 1)
        quads((0, 3))
        for d in (4, 5, 6, 7, 0, 1):
            guarded(there(*SIDES[d]), quad_copy(it, d).start)
        lax.fori_loop(HALO, ROWS - HALO, pack, 0, unroll=ROWS - 2 * HALO if it else 1)
        quads((1, 2))
        for d in (2, 3):
            guarded(there(*SIDES[d]), quad_copy(it, d).start)

    res_copy.wait()

    def spread(l, carry):
        v = res[l]
        a0[pl.ds(HALO * LEV + l, 8, stride=LEV), :] = v[0:8]
        a0[pl.ds((HALO + 8) * LEV + l, 8, stride=LEV), :] = v[8:16]
        return carry

    lax.fori_loop(0, LEV, spread, 0, unroll=4)
    for half in range(HALVES):
        send_rows(0, half)
    send_halos(0)
    for i, c in ORDER[FIRST:]:
        member_copy(i, c).start()

    for copy in wind_copies:
        copy.wait()

    def coefficients(l, carry):
        wx, wy = wx_ref[l], wy_ref[l]
        c0[pl.ds(l, 1), :] = jnp.full((1, COLS), (1.0 - 4.0 * diffusion - wx - wy) / diffusion, F32)
        ax[pl.ds(l, 1), :] = jnp.full((1, COLS), (diffusion + wx) / diffusion, F32)
        ay[pl.ds(l, 1), :] = jnp.full((1, COLS), (diffusion + wy) / diffusion, F32)
        return carry

    lax.fori_loop(0, LEV, coefficients, 0)

    total_w = sum(1.0 - (i / 17.0) ** 2 for i in range(-16, 17))
    source = lax.broadcasted_iota(jnp.int32, (COLS, COLS), 0)
    target = lax.broadcasted_iota(jnp.int32, (COLS, COLS), 1)
    together = source // 16 == target // 16
    for which, k, near in (
        (0, source - target, None),
        (1, source - 16 - target, together),
        (2, source + 16 - target, together),
    ):
        kf = k.astype(F32)
        reached = jnp.abs(k) <= REACH
        if near is not None:
            reached = jnp.logical_and(reached, near)
        full = jnp.where(reached, (1.0 - kf * kf * (1.0 / 289.0)) * (1.0 / total_w), 0.0)
        coarse = full.astype(BF16)
        band[which, 0] = coarse
        band[which, 1] = (full - coarse.astype(F32)).astype(BF16)

    def strip_coefficient(ref):
        total = jnp.zeros((8, COLS), F32)
        for k in range(GROUPS):
            total = jnp.where(group == k, ref[8 * k : 8 * k + 8, :], total)
        return total

    row_low = jnp.where(t > 0, 1.0, 0.0).astype(F32)
    row_high = jnp.where(t < tiles - 1, 1.0, 0.0).astype(F32)
    inside = jnp.logical_and(
        jnp.logical_or(q >= 4, m > 0), jnp.logical_or(q < 12, m < blocks - 1)
    )
    strip_mask = jnp.where(inside, 1.0, 0.0).astype(F32)

    binomial = (1.0, 4.0, 6.0, 4.0, 1.0)

    def column_powers(a, r, most):
        for k in range(GROUPS):
            here = pl.ds(pl.multiple_of(r * LEV + 8 * k, 8), 8)
            x = a[here, :]
            for power in range(1, most + 1):
                left = jnp.where(lane == 0, 0.0, pltpu.roll(x, 1, 1))
                right = jnp.where(lane == COLS - 1, 0.0, pltpu.roll(x, COLS - 1, 1))
                x = left + ay[8 * k : 8 * k + 8, :] * right
                powers[power - 1, here, :] = x

    def adjoint_early(it):
        def row(r, carry):
            column_powers((a0, a1)[it], r, STEPS)
            return carry

        lax.fori_loop(HALO, HALO + ROWS, row, 0, unroll=2 if it else 1)
        for stage in range(1, STEPS + 1):
            lax.fori_loop(
                HALO + stage, HALO + ROWS - stage, functools.partial(row_stage, it, stage), 0,
                unroll=2 if it else 1,
            )

    def row_stage(it, stage, r, carry, scale=None):
        src = ((a0, a1)[it], w1, w2, w3)[stage - 1]
        dst = (w1, w2, w3, gt)[stage - 1]
        for k in range(GROUPS):
            at = r * LEV + 8 * k
            here = pl.ds(pl.multiple_of(at, 8), 8)
            s = slice(8 * k, 8 * k + 8)
            out = (
                c0[s, :] * src[here, :]
                + src[pl.ds(pl.multiple_of(at - LEV, 8), 8), :]
                + ax[s, :] * src[pl.ds(pl.multiple_of(at + LEV, 8), 8), :]
            )
            side = powers[stage - 1, here, :]
            out = out + (side if stage == STEPS else binomial[stage] * side)
            if scale is not None:
                out = out * scale
            if stage == STEPS:
                dst[pl.ds(pl.multiple_of(at - HALO * LEV, 8), 8), :] = out
            else:
                dst[here, :] = out
        return carry

    def adjoint_late(it):
        a = (a0, a1)[it]
        receive_rows(it)
        for r in range(1, HALO):
            column_powers(a, r, r)
            column_powers(a, XROWS - 1 - r, r)
        for stage in range(1, STEPS + 1):
            for r in range(stage, HALO + stage):
                row_stage(it, stage, r, 0, row_low if r < HALO else None)
                r = XROWS - 1 - r
                row_stage(it, stage, r, 0, row_high if r >= HALO + ROWS else None)

        for d in range(8):
            dt, dm = SIDES[d]
            guarded(there(-dt, -dm), quad_copy(it, d).wait_recv)
        for r in range(XROWS):
            left = pltpu.roll(ql[it, r // 4], (-4 * (r % 4)) % COLS, 1)
            right = pltpu.roll(qr[it, r // 4], (12 - 4 * (r % 4)) % COLS, 1)
            strip[0, r] = jnp.where(q < 4, left, jnp.where(q >= 12, right, own[it, r]))
        sc0, sax, say = strip_coefficient(c0), strip_coefficient(ax), strip_coefficient(ay)
        mine = jnp.logical_and(q >= 4, q < 12)

        def strip_step(load, r):
            v = load(r)
            out = (
                sc0 * v
                + (load(r - 1) + pltpu.roll(v, 1, 1))
                + sax * load(r + 1)
                + say * pltpu.roll(v, COLS - 1, 1)
            )
            return out * row_low if r < HALO else out * row_high if r >= HALO + ROWS else out

        for step in range(1, STEPS + 1):

            def joined(r):
                outer = strip[step - 1, r]
                return jnp.where(mine, 0.0 if step == 1 else sides[step - 2, r], outer)

            for r in range(step, XROWS - step):
                sides[step - 1, r] = strip_step(joined, r)
                if step < STEPS:
                    strip[step, r] = strip_step(lambda i: strip[step - 1, i], r) * strip_mask

        def finish(r, carry):
            v = sides[STEPS - 1, HALO + r]
            v = jnp.where(q < 4, pltpu.roll(v, COLS - 8, 1), v)
            for k in range(GROUPS):
                here = pl.ds(pl.multiple_of(r * LEV + 8 * k, 8), 8)
                ends = jnp.where(
                    jnp.logical_or(lane < HALO, lane >= COLS - HALO),
                    pltpu.roll(v, COLS - HALO - 16 * k, 1),
                    0.0,
                )
                out = (gt[here, :] + ends) * diffusion**STEPS
                g[pl.ds(8 * k * ROWS + r, 8, stride=ROWS), :] = out.astype(BF16).astype(F32)
            return carry

        lax.fori_loop(0, ROWS, finish, 0, unroll=4 if it else 1)

    own_rows = pl.ds(REACH, ROWS)

    def project(it, pair, first, count, fresh):
        if fresh:
            start = (jnp.zeros((ROWS, COLS), F32), jnp.zeros((ROWS, COLS), F32))
        else:
            start = (proj[it, 2 * pair, own_rows, :], proj[it, 2 * pair + 1, own_rows, :])

        def level(l, sums):
            v = g[pl.ds(pl.multiple_of(l * ROWS, ROWS), ROWS), :]
            return tuple(s + mt[pair, n, l].astype(F32) * v for n, s in enumerate(sums))

        sums = lax.fori_loop(first, first + count, level, start, unroll=8)
        for n in range(2):
            proj[it, 2 * pair + n, own_rows, :] = sums[n]

    def project_copy(it, pair, slot, d):
        return pltpu.make_async_remote_copy(
            src_ref=proj_out.at[it, pl.ds(2 * pair, 2)],
            dst_ref=proj_in.at[it, d, pl.ds(2 * pair, 2)],
            send_sem=p_send.at[it, slot, d], recv_sem=p_recv.at[it, slot, d],
            device_id=peer(*SIDES[d]), device_id_type=MESH,
        )

    order = ([m] + [mate(-dy, dz) for dy, dz in FLOWS], list(range(8)))

    def send_project(it, slot):
        for n in range(2):
            member = 2 * order[it][slot] + n
            proj_out[it, member] = proj[it, member, own_rows, :].astype(BF16)
        for d in (0, 1):
            guarded(there(*SIDES[d]), project_copy(it, order[it][slot], slot, d).start)

    def taper(ref, lead, at):
        total = w[REACH] * ref[(*lead, pl.ds(at, 8), slice(None))]
        for k in range(1, REACH + 1):
            total = total + w[REACH + k] * (
                ref[(*lead, pl.ds(at - k, 8), slice(None))]
                + ref[(*lead, pl.ds(at + k, 8), slice(None))]
            )
        return total

    def smooth_rows(it, slot):
        pair = order[it][slot]
        for d in (0, 1):

            def unpack(d=d):
                project_copy(it, pair, slot, d).wait_recv()
                for n in range(2):
                    proj[it, 2 * pair + n, pl.ds(0 if d == 0 else REACH + ROWS, REACH), :] = proj_in[
                        it, d, 2 * pair + n
                    ].astype(F32)

            dt, dm = SIDES[d]
            guarded(there(-dt, -dm), unpack)
        for n in range(2):
            for half in (0, 8):
                sx[pl.ds(pl.multiple_of((2 * pair + n) * ROWS + half, 8), 8), :] = taper(
                    proj, (it, 2 * pair + n), REACH + half
                )

    def column_copy(it, d, part):
        dt, dm = COLUMN_SIDES[d]
        src, dst = (pk_r, cl_in) if dm > 0 else (pk_l, cr_in)
        return pltpu.make_async_remote_copy(
            src_ref=src.at[it, part],
            dst_ref=dst.at[it, part, column_place(dt)],
            send_sem=c_send.at[it, d, part], recv_sem=c_recv.at[it, d, part],
            device_id=peer(dt, dm), device_id_type=MESH,
        )

    def column_place(dt):
        return 1 if dt == 0 else 0 if dt > 0 else 2

    def send_columns(it, part):
        rights, lefts = [], []
        for half in (0, 8):
            right = jnp.zeros((8, COLS), F32)
            left = jnp.zeros((8, COLS), F32)
            for n in range(8):
                v = proj[it, 8 * part + n, REACH + half : REACH + half + 8, :]
                right = jnp.where(group == n, pltpu.roll(v, (16 * n - 112) % COLS, 1), right)
                left = jnp.where(group == n, pltpu.roll(v, 16 * n, 1), left)
            rights.append(right)
            lefts.append(left)
        pk_r[it, part] = jnp.concatenate(rights).astype(BF16)
        pk_l[it, part] = jnp.concatenate(lefts).astype(BF16)
        for d, side in enumerate(COLUMN_SIDES):
            guarded(there(*side), column_copy(it, d, part).start)

    def receive_columns(it):
        for d, (dt, dm) in enumerate(COLUMN_SIDES):

            def unpack(d=d, dt=dt, dm=dm):
                place = column_place(dt)
                got, to = (cl_in, cl) if dm > 0 else (cr_in, cr)
                for part in range(2):
                    column_copy(it, d, part).wait_recv()
                    to[it, part, place * REACH : (place + 1) * REACH, :] = got[
                        it, part, place
                    ].astype(F32)

            guarded(there(-dt, -dm), unpack)

    def split(x):
        high = x.astype(BF16)
        return high, (x - high.astype(F32)).astype(BF16)

    def times(x, which):
        high, low = split(x)
        dot = functools.partial(jnp.dot, preferred_element_type=F32)
        return dot(high, band[which, 0]) + (dot(low, band[which, 0]) + dot(high, band[which, 1]))

    def smooth_columns(it):
        z[...] = times(sx[...], 0)
        receive_columns(it)
        outer = []
        for which, ref in ((1, cl), (2, cr)):
            x = jnp.concatenate(
                [taper(ref, (it, part), REACH + half) for part in range(2) for half in (0, 8)]
            )
            outer.append(times(x, which))
        for part in range(2):
            for half in (0, 8):
                at = part * ROWS + half
                from_left, from_right = (x[at : at + 8, :] for x in outer)
                for n in range(8):
                    to = (8 * part + n) * ROWS + half
                    z[to : to + 8, :] = z[to : to + 8, :] + jnp.where(
                        lane < 16,
                        pltpu.roll(from_left, (-16 * n) % COLS, 1),
                        jnp.where(
                            lane >= 112, pltpu.roll(from_right, (112 - 16 * n) % COLS, 1), 0.0
                        ),
                    )

    def out_copy(part):
        levels = pl.ds(part * (LEV // PARTS), LEV // PARTS)
        return pltpu.make_async_copy(half_ref.at[levels], out_hbm.at[levels], out_sem.at[part])

    def increments(it):
        width = 4

        def levels(step, carry):
            sums = [jnp.zeros((ROWS, COLS), F32) for _ in range(width)]
            for pair in range(8):
                for n in range(2):
                    v = z[pl.ds((2 * pair + n) * ROWS, ROWS), :]
                    for i in range(width):
                        sums[i] = sums[i] + mt[pair, n, width * step + i].astype(F32) * v
            for i in range(width):
                l = width * step + i
                if it == 0:
                    half = relax * sums[i]
                    half_ref[l] = half
                    v = res[l] - half
                    a1[pl.ds(HALO * LEV + l, 8, stride=LEV), :] = v[0:8]
                    a1[pl.ds((HALO + 8) * LEV + l, 8, stride=LEV), :] = v[8:16]
                else:
                    half_ref[l] = half_ref[l] + relax * sums[i]
            return carry

        parts = PARTS if it else HALVES
        for part in range(parts):
            count = LEV // parts // width
            lax.fori_loop(part * count, (part + 1) * count, levels, 0)
            if it == 0:
                send_rows(1, part)
            else:
                out_copy(part).start()

    def halos_sent(it):
        for d in (0, 1):
            for half in range(HALVES):
                guarded(there(*SIDES[d]), row_copy(it, d, half).wait_send)
        for d in range(8):
            guarded(there(*SIDES[d]), quad_copy(it, d).wait_send)

    def projects_sent(it):
        for slot in range(8):
            for d in (0, 1):
                guarded(there(*SIDES[d]), project_copy(it, order[it][slot], slot, d).wait_send)

    def columns_sent(it):
        for d, side in enumerate(COLUMN_SIDES):
            for part in range(2):
                guarded(there(*side), column_copy(it, d, part).wait_send)

    adjoint_early(0)
    adjoint_late(0)
    own_copy.wait()
    project(0, order[0][0], 0, LEV, True)
    send_project(0, 0)
    for i, c in ORDER:
        member_copy(i, c).wait_recv()
        project(0, order[0][1 + i], c * CLEV, CLEV, c == 0)
        if c == CHUNKS - 1:
            send_project(0, 1 + i)
    for part in range(2):
        send_columns(0, part)
    for slot in range(8):
        smooth_rows(0, slot)
    smooth_columns(0)
    increments(0)

    send_halos(1)
    adjoint_early(1)
    for i, c in ORDER:
        member_copy(i, c).wait_send()
    halos_sent(0)
    projects_sent(0)
    columns_sent(0)
    adjoint_late(1)
    for slot in range(8):
        project(1, slot, 0, LEV, True)
        send_project(1, slot)
        if slot % 4 == 3:
            send_columns(1, slot // 4)
    halos_sent(1)
    for slot in range(8):
        smooth_rows(1, slot)
    projects_sent(1)
    smooth_columns(1)
    increments(1)
    columns_sent(1)
    for part in range(PARTS):
        out_copy(part).wait()


def per_device(tiles, blocks, residual_in, members, wind_x, wind_y):
    vmem = pltpu.VMEM
    dma = lambda *shape: pltpu.SemaphoreType.DMA(shape)
    anywhere = pl.BlockSpec(memory_space=pl.ANY)
    extended = vmem((XROWS * LEV, COLS), F32)
    coefficient = vmem((LEV, COLS), F32)
    half = pl.pallas_call(
        functools.partial(kernel, tiles, blocks),
        out_shape=jax.ShapeDtypeStruct((LEV, ROWS, COLS), F32),
        in_specs=[anywhere] * 4,
        out_specs=anywhere,
        scratch_shapes=[
            vmem((LEV, ROWS, COLS), F32),
            vmem((8, 2, LEV, ROWS, COLS), BF16),
            extended, extended, extended, extended, extended,
            coefficient, coefficient, coefficient,
            vmem((2, XROWS, 8, COLS), F32),
            vmem((STEPS, XROWS, 8, COLS), F32),
            vmem((STEPS, XROWS, 8, COLS), F32),
            vmem((STEPS, XROWS * LEV, COLS), F32),
            vmem((2, 4, 8, COLS), F32), vmem((2, 4, 8, COLS), F32),
            vmem((2, 6, 8, COLS), F32), vmem((2, 6, 8, COLS), F32),
            vmem((ROWS * LEV, COLS), F32),
            vmem((LEV * ROWS, COLS), F32),
            vmem((2, 2, HALVES, HALO * HLEV, COLS), BF16),
            vmem((2, 2, HALVES, HALO * HLEV, COLS), BF16),
            vmem((2, 16, ROWS + 2 * REACH, COLS), F32),
            vmem((2, 16, ROWS, COLS), BF16),
            vmem((2, 2, 16, REACH, COLS), BF16),
            vmem((16 * ROWS, COLS), F32),
            vmem((2, 2, ROWS, COLS), BF16), vmem((2, 2, ROWS, COLS), BF16),
            vmem((2, 2, 3, REACH, COLS), BF16),
            vmem((2, 2, 3, REACH, COLS), BF16),
            vmem((2, 2, ROWS + 2 * REACH, COLS), F32),
            vmem((2, 2, ROWS + 2 * REACH, COLS), F32),
            vmem((3, 2, COLS, COLS), BF16),
            vmem((16 * ROWS, COLS), F32),
            vmem((LEV, ROWS, COLS), F32),
            pltpu.SMEM((LEV,), F32), pltpu.SMEM((LEV,), F32),
            pltpu.SemaphoreType.DMA, pltpu.SemaphoreType.DMA, dma(2), dma(PARTS),
            dma(len(FLOWS), CHUNKS), dma(len(FLOWS), CHUNKS),
            dma(2, 8), dma(2, 8),
            dma(2, 2, HALVES), dma(2, 2, HALVES),
            dma(2, 8, 2), dma(2, 8, 2),
            dma(2, len(COLUMN_SIDES), 2), dma(2, len(COLUMN_SIDES), 2),
        ],
        compiler_params=pltpu.CompilerParams(collective_id=0, has_side_effects=True),
        name="ensemble_step",
    )(residual_in, members, wind_x, wind_y)
    return (half * (1.0 / relax), residual_in - half)


def solution(mesh):
    return jax.shard_map(
        functools.partial(per_device, mesh.shape["tile"], mesh.shape["member"]),
        mesh=mesh,
        in_specs=(P(None, "tile", "member"), P("member", None, "tile", None), P(), P()),
        out_specs=(P(None, "tile", "member"), P(None, "tile", "member")),
        check_vma=False,
    )
```

```python
import functools

import jax
import jax.numpy as jnp
from jax import lax
from jax.experimental import pallas as pl
from jax.experimental.pallas import tpu as pltpu
from jax.sharding import PartitionSpec as P

MESH = pl.DeviceIdType.MESH
F32 = jnp.float32
BF16 = jnp.bfloat16

LEV = 64
ROWS = 16
COLS = 128
GROUPS = LEV // 8
STEPS = 4
HALO = STEPS
XROWS = ROWS + 2 * HALO
REACH = 16
CHUNKS = 8
CLEV = LEV // CHUNKS

diffusion = 0.1
relax = 0.5

FLOWS = ((2, 1), (0, 1), (2, 0), (1, 1), (3, 1), (1, 0), (3, 0))
ORDER = [(i, c) for c in range(CHUNKS) for i in (0, 1, 2)]
ORDER += [(i, c) for c in range(CHUNKS) for i in (3, 4, 5, 6)]
FIRST = 6
HALVES = 2
HLEV = LEV // HALVES
PARTS = 4
SIDES = ((1, 0), (-1, 0), (0, 1), (0, -1), (1, 1), (-1, 1), (1, -1), (-1, -1))


COLUMN_SIDES = ((1, 1), (-1, 1), (1, -1), (-1, -1), (0, 1), (0, -1))


def taper_weights():
    raw = [1.0 - (k / 17.0) ** 2 for k in range(-16, 17)]
    total = sum(raw)
    return [value / total for value in raw]


def kernel(
    tiles, blocks,
    res_hbm, mem_hbm, wx_hbm, wy_hbm,
    out_hbm,
    res, mt, a0, a1, w1, w2, w3, c0, ax, ay, own, strip, sides, powers, mr, ml, ql, qr, gt, g,
    row_out, row_in, proj, proj_out, proj_in, sx, pk_r, pk_l, cl_in, cr_in, cl, cr, band, z, half_ref,
    wx_ref, wy_ref, own_sem, res_sem, wind_sem, out_sem, m_send, m_recv, h_send, h_recv, r_send, r_recv, p_send, p_recv, c_send, c_recv,
):
    t = lax.axis_index("tile")
    m = lax.axis_index("member")
    zh, y = m // 4, m % 4
    w = taper_weights()

    def there(dt, dm):
        ok = None
        for cond in ([t < tiles - 1] if dt > 0 else [t > 0] if dt < 0 else []) + (
            [m < blocks - 1] if dm > 0 else [m > 0] if dm < 0 else []
        ):
            ok = cond if ok is None else jnp.logical_and(ok, cond)
        return ok

    def peer(dt, dm):
        return ((t + dt + tiles) % tiles, (m + dm + blocks) % blocks)

    def mate(dy, dz):
        return ((zh + dz) % 2) * 4 + (y + dy + 4) % 4

    res_copy = pltpu.make_async_copy(res_hbm, res, res_sem)
    res_copy.start()
    wind_copies = [
        pltpu.make_async_copy(wind, wind_ref, wind_sem.at[n])
        for n, (wind, wind_ref) in enumerate(((wx_hbm, wx_ref), (wy_hbm, wy_ref)))
    ]
    for copy in wind_copies:
        copy.start()
    own_copy = pltpu.make_async_copy(
        mem_hbm.at[:, :, :, pl.ds(pl.multiple_of(m * COLS, COLS), COLS)], mt.at[m], own_sem
    )
    own_copy.start()

    barrier = pltpu.get_barrier_semaphore()
    count = jnp.int32(len(FLOWS))
    for dy, dz in FLOWS:
        pl.semaphore_signal(barrier, inc=1, device_id=(t, mate(dy, dz)), device_id_type=MESH)
    for dt, dm in SIDES:
        if dt == 0:
            continue
        ok = there(dt, dm)
        count = count + ok.astype(jnp.int32)

        @pl.when(ok)
        def _():
            pl.semaphore_signal(barrier, inc=1, device_id=peer(dt, dm), device_id_type=MESH)

    pl.semaphore_wait(barrier, count)

    def member_copy(i, c):
        dy, dz = FLOWS[i]
        target = mate(dy, dz)
        return pltpu.make_async_remote_copy(
            src_ref=mem_hbm.at[
                :, pl.ds(c * CLEV, CLEV), :, pl.ds(pl.multiple_of(target * COLS, COLS), COLS)
            ],
            dst_ref=mt.at[m, :, pl.ds(c * CLEV, CLEV)],
            send_sem=m_send.at[i, c],
            recv_sem=m_recv.at[i, c],
            device_id=(t, target),
            device_id_type=MESH,
        )

    for i, c in ORDER[:FIRST]:
        member_copy(i, c).start()

    @pl.when(t == 0)
    def _():
        for a in (a0, a1):
            a[pl.ds(0, HALO * LEV), :] = jnp.zeros((HALO * LEV, COLS), F32)
        own[:, 0:HALO] = jnp.zeros((2, HALO, 8, COLS), F32)
        ql[:, 0] = jnp.zeros((2, 8, COLS), F32)
        qr[:, 0] = jnp.zeros((2, 8, COLS), F32)
        proj[:, :, 0:REACH, :] = jnp.zeros((2, 16, REACH, COLS), F32)
        cl[:, :, 0:REACH, :] = jnp.zeros((2, 2, REACH, COLS), F32)
        cr[:, :, 0:REACH, :] = jnp.zeros((2, 2, REACH, COLS), F32)

    @pl.when(t == tiles - 1)
    def _():
        for a in (a0, a1):
            a[pl.ds((HALO + ROWS) * LEV, HALO * LEV), :] = jnp.zeros((HALO * LEV, COLS), F32)
        own[:, HALO + ROWS :] = jnp.zeros((2, HALO, 8, COLS), F32)
        ql[:, 5] = jnp.zeros((2, 8, COLS), F32)
        qr[:, 5] = jnp.zeros((2, 8, COLS), F32)
        proj[:, :, REACH + ROWS :, :] = jnp.zeros((2, 16, REACH, COLS), F32)
        cl[:, :, REACH + ROWS :, :] = jnp.zeros((2, 2, REACH, COLS), F32)
        cr[:, :, REACH + ROWS :, :] = jnp.zeros((2, 2, REACH, COLS), F32)

    @pl.when(m == 0)
    def _():
        ql[...] = jnp.zeros(ql.shape, F32)
        cl[...] = jnp.zeros(cl.shape, F32)

    @pl.when(m == blocks - 1)
    def _():
        qr[...] = jnp.zeros(qr.shape, F32)
        cr[...] = jnp.zeros(cr.shape, F32)

    lane = lax.broadcasted_iota(jnp.int32, (8, COLS), 1)
    q = lane % 16
    group = lane // 16

    def row_copy(it, d, half):
        return pltpu.make_async_remote_copy(
            src_ref=row_out.at[it, d, half], dst_ref=row_in.at[it, d, half],
            send_sem=r_send.at[it, d, half], recv_sem=r_recv.at[it, d, half],
            device_id=peer(*SIDES[d]), device_id_type=MESH,
        )

    def send_rows(it, half):
        a = (a0, a1)[it]
        for d, first in ((0, ROWS), (1, HALO)):
            for r in range(HALO):
                row_out[it, d, half, r * HLEV : (r + 1) * HLEV, :] = a[
                    (first + r) * LEV + half * HLEV : (first + r) * LEV + (half + 1) * HLEV, :
                ].astype(BF16)
            guarded(there(*SIDES[d]), row_copy(it, d, half).start)

    def receive_rows(it):
        a = (a0, a1)[it]
        for d, first in ((0, 0), (1, HALO + ROWS)):

            def unpack(d=d, first=first):
                for half in range(HALVES):
                    row_copy(it, d, half).wait_recv()
                    for r in range(HALO):
                        at = (first + r) * LEV + half * HLEV
                        a[at : at + HLEV, :] = row_in[
                            it, d, half, r * HLEV : (r + 1) * HLEV, :
                        ].astype(F32)

            dt, dm = SIDES[d]
            guarded(there(-dt, -dm), unpack)

    def quad_copy(it, d):
        dt, dm = SIDES[d]
        src, dst = (mr.at[it], ql.at[it]) if dm > 0 else (ml.at[it], qr.at[it])
        if dm == 0:
            src = own.at[it, pl.ds(ROWS if dt > 0 else HALO, HALO)]
            dst = own.at[it, pl.ds(0 if dt > 0 else HALO + ROWS, HALO)]
        elif dt == 0:
            src, dst = src, dst.at[pl.ds(1, 4)]
        elif dt > 0:
            src, dst = src.at[pl.ds(3, 1)], dst.at[pl.ds(0, 1)]
        else:
            src, dst = src.at[pl.ds(0, 1)], dst.at[pl.ds(5, 1)]
        return pltpu.make_async_remote_copy(
            src_ref=src, dst_ref=dst, send_sem=h_send.at[it, d], recv_sem=h_recv.at[it, d],
            device_id=peer(dt, dm), device_id_type=MESH,
        )

    def guarded(ok, action):
        if ok is None:
            action()
        else:
            pl.when(ok)(action)

    def edges(a, r):
        total = jnp.zeros((8, COLS), F32)
        for k in range(GROUPS):
            v = a[pl.ds(pl.multiple_of(r * LEV + 8 * k, 8), 8), :]
            low = pltpu.roll(v, (16 * k + 4) % COLS, 1)
            high = pltpu.roll(v, (16 * k + 12) % COLS, 1)
            part = jnp.where(q < 8, low, high)
            total = jnp.where(group == k, part, total)
        return total

    def send_halos(it):
        a = (a0, a1)[it]

        def pack(r, carry):
            own[it, HALO + r] = edges(a, HALO + r)
            return carry

        def pack_ends(r, carry):
            return pack(r + ROWS - HALO, pack(r, carry))

        def quads(numbers):
            for quad in numbers:
                right = jnp.zeros((8, COLS), F32)
                left = jnp.zeros((8, COLS), F32)
                for k in range(4):
                    v = own[it, HALO + 4 * quad + k]
                    here = q // 4 == k
                    right = jnp.where(here, pltpu.roll(v, (4 * k - 8) % COLS, 1), right)
                    left = jnp.where(here, pltpu.roll(v, (4 * k - 4) % COLS, 1), left)
                mr[it, quad] = right
                ml[it, quad] = left

        lax.fori_loop(0, HALO, pack_ends, 0, unroll=HALO if it else 1)
        quads((0, 3))
        for d in (4, 5, 6, 7, 0, 1):
            guarded(there(*SIDES[d]), quad_copy(it, d).start)
        lax.fori_loop(HALO, ROWS - HALO, pack, 0, unroll=ROWS - 2 * HALO if it else 1)
        quads((1, 2))
        for d in (2, 3):
            guarded(there(*SIDES[d]), quad_copy(it, d).start)

    res_copy.wait()

    def spread(l, carry):
        v = res[l]
        a0[pl.ds(HALO * LEV + l, 8, stride=LEV), :] = v[0:8]
        a0[pl.ds((HALO + 8) * LEV + l, 8, stride=LEV), :] = v[8:16]
        return carry

    lax.fori_loop(0, LEV, spread, 0, unroll=4)
    for half in range(HALVES):
        send_rows(0, half)
    send_halos(0)
    for i, c in ORDER[FIRST:]:
        member_copy(i, c).start()

    for copy in wind_copies:
        copy.wait()

    def coefficients(l, carry):
        wx, wy = wx_ref[l], wy_ref[l]
        c0[pl.ds(l, 1), :] = jnp.full((1, COLS), (1.0 - 4.0 * diffusion - wx - wy) / diffusion, F32)
        ax[pl.ds(l, 1), :] = jnp.full((1, COLS), (diffusion + wx) / diffusion, F32)
        ay[pl.ds(l, 1), :] = jnp.full((1, COLS), (diffusion + wy) / diffusion, F32)
        return carry

    lax.fori_loop(0, LEV, coefficients, 0)

    total_w = sum(1.0 - (i / 17.0) ** 2 for i in range(-16, 17))
    source = lax.broadcasted_iota(jnp.int32, (COLS, COLS), 0)
    target = lax.broadcasted_iota(jnp.int32, (COLS, COLS), 1)
    together = source // 16 == target // 16
    for which, k, near in (
        (0, source - target, None),
        (1, source - 16 - target, together),
        (2, source + 16 - target, together),
    ):
        kf = k.astype(F32)
        reached = jnp.abs(k) <= REACH
        if near is not None:
            reached = jnp.logical_and(reached, near)
        full = jnp.where(reached, (1.0 - kf * kf * (1.0 / 289.0)) * (1.0 / total_w), 0.0)
        coarse = full.astype(BF16)
        band[which, 0] = coarse
        band[which, 1] = (full - coarse.astype(F32)).astype(BF16)

    def strip_coefficient(ref):
        total = jnp.zeros((8, COLS), F32)
        for k in range(GROUPS):
            total = jnp.where(group == k, ref[8 * k : 8 * k + 8, :], total)
        return total

    row_low = jnp.where(t > 0, 1.0, 0.0).astype(F32)
    row_high = jnp.where(t < tiles - 1, 1.0, 0.0).astype(F32)
    inside = jnp.logical_and(
        jnp.logical_or(q >= 4, m > 0), jnp.logical_or(q < 12, m < blocks - 1)
    )
    strip_mask = jnp.where(inside, 1.0, 0.0).astype(F32)

    binomial = (1.0, 4.0, 6.0, 4.0, 1.0)

    def column_powers(a, r, most):
        for k in range(GROUPS):
            here = pl.ds(pl.multiple_of(r * LEV + 8 * k, 8), 8)
            x = a[here, :]
            for power in range(1, most + 1):
                left = jnp.where(lane == 0, 0.0, pltpu.roll(x, 1, 1))
                right = jnp.where(lane == COLS - 1, 0.0, pltpu.roll(x, COLS - 1, 1))
                x = left + ay[8 * k : 8 * k + 8, :] * right
                powers[power - 1, here, :] = x

    def adjoint_early(it):
        def row(r, carry):
            column_powers((a0, a1)[it], r, STEPS)
            return carry

        lax.fori_loop(HALO, HALO + ROWS, row, 0, unroll=2 if it else 1)
        for stage in range(1, STEPS + 1):
            lax.fori_loop(
                HALO + stage, HALO + ROWS - stage, functools.partial(row_stage, it, stage), 0,
                unroll=2 if it else 1,
            )

    def row_stage(it, stage, r, carry, scale=None):
        src = ((a0, a1)[it], w1, w2, w3)[stage - 1]
        dst = (w1, w2, w3, gt)[stage - 1]
        for k in range(GROUPS):
            at = r * LEV + 8 * k
            here = pl.ds(pl.multiple_of(at, 8), 8)
            s = slice(8 * k, 8 * k + 8)
            out = (
                c0[s, :] * src[here, :]
                + src[pl.ds(pl.multiple_of(at - LEV, 8), 8), :]
                + ax[s, :] * src[pl.ds(pl.multiple_of(at + LEV, 8), 8), :]
            )
            side = powers[stage - 1, here, :]
            out = out + (side if stage == STEPS else binomial[stage] * side)
            if scale is not None:
                out = out * scale
            if stage == STEPS:
                dst[pl.ds(pl.multiple_of(at - HALO * LEV, 8), 8), :] = out
            else:
                dst[here, :] = out
        return carry

    def adjoint_late(it):
        a = (a0, a1)[it]
        receive_rows(it)
        for r in range(1, HALO):
            column_powers(a, r, r)
            column_powers(a, XROWS - 1 - r, r)
        for stage in range(1, STEPS + 1):
            for r in range(stage, HALO + stage):
                row_stage(it, stage, r, 0, row_low if r < HALO else None)
                r = XROWS - 1 - r
                row_stage(it, stage, r, 0, row_high if r >= HALO + ROWS else None)

        for d in range(8):
            dt, dm = SIDES[d]
            guarded(there(-dt, -dm), quad_copy(it, d).wait_recv)
        for r in range(XROWS):
            left = pltpu.roll(ql[it, r // 4], (-4 * (r % 4)) % COLS, 1)
            right = pltpu.roll(qr[it, r // 4], (12 - 4 * (r % 4)) % COLS, 1)
            strip[0, r] = jnp.where(q < 4, left, jnp.where(q >= 12, right, own[it, r]))
        sc0, sax, say = strip_coefficient(c0), strip_coefficient(ax), strip_coefficient(ay)
        mine = jnp.logical_and(q >= 4, q < 12)

        def strip_step(load, r):
            v = load(r)
            out = (
                sc0 * v
                + (load(r - 1) + pltpu.roll(v, 1, 1))
                + sax * load(r + 1)
                + say * pltpu.roll(v, COLS - 1, 1)
            )
            return out * row_low if r < HALO else out * row_high if r >= HALO + ROWS else out

        for step in range(1, STEPS + 1):

            def joined(r):
                outer = strip[step - 1, r]
                return jnp.where(mine, 0.0 if step == 1 else sides[step - 2, r], outer)

            for r in range(step, XROWS - step):
                sides[step - 1, r] = strip_step(joined, r)
                if step < STEPS:
                    strip[step, r] = strip_step(lambda i: strip[step - 1, i], r) * strip_mask

        def finish(r, carry):
            v = sides[STEPS - 1, HALO + r]
            v = jnp.where(q < 4, pltpu.roll(v, COLS - 8, 1), v)
            for k in range(GROUPS):
                here = pl.ds(pl.multiple_of(r * LEV + 8 * k, 8), 8)
                ends = jnp.where(
                    jnp.logical_or(lane < HALO, lane >= COLS - HALO),
                    pltpu.roll(v, COLS - HALO - 16 * k, 1),
                    0.0,
                )
                out = (gt[here, :] + ends) * diffusion**STEPS
                g[pl.ds(8 * k * ROWS + r, 8, stride=ROWS), :] = out.astype(BF16).astype(F32)
            return carry

        lax.fori_loop(0, ROWS, finish, 0, unroll=4 if it else 1)

    own_rows = pl.ds(REACH, ROWS)

    def project(it, pair, first, count, fresh):
        if fresh:
            start = (jnp.zeros((ROWS, COLS), F32), jnp.zeros((ROWS, COLS), F32))
        else:
            start = (proj[it, 2 * pair, own_rows, :], proj[it, 2 * pair + 1, own_rows, :])

        def level(l, sums):
            v = g[pl.ds(pl.multiple_of(l * ROWS, ROWS), ROWS), :]
            return tuple(s + mt[pair, n, l].astype(F32) * v for n, s in enumerate(sums))

        sums = lax.fori_loop(first, first + count, level, start, unroll=8)
        for n in range(2):
            proj[it, 2 * pair + n, own_rows, :] = sums[n]

    def project_both(it, pair):
        def level(l, sums):
            v = g[pl.ds(pl.multiple_of(l * ROWS, ROWS), ROWS), :]
            return tuple(
                s + mt[pair + n // 2, n % 2, l].astype(F32) * v for n, s in enumerate(sums)
            )

        sums = lax.fori_loop(
            0, LEV, level, tuple(jnp.zeros((ROWS, COLS), F32) for _ in range(4)), unroll=8
        )
        for n in range(4):
            proj[it, 2 * pair + n, own_rows, :] = sums[n]

    def project_copy(it, pair, slot, d):
        return pltpu.make_async_remote_copy(
            src_ref=proj_out.at[it, pl.ds(2 * pair, 2)],
            dst_ref=proj_in.at[it, d, pl.ds(2 * pair, 2)],
            send_sem=p_send.at[it, slot, d], recv_sem=p_recv.at[it, slot, d],
            device_id=peer(*SIDES[d]), device_id_type=MESH,
        )

    order = ([m] + [mate(-dy, dz) for dy, dz in FLOWS], list(range(8)))

    def send_project(it, slot):
        for n in range(2):
            member = 2 * order[it][slot] + n
            proj_out[it, member] = proj[it, member, own_rows, :].astype(BF16)
        for d in (0, 1):
            guarded(there(*SIDES[d]), project_copy(it, order[it][slot], slot, d).start)

    def taper(ref, lead, at):
        total = w[REACH] * ref[(*lead, pl.ds(at, 8), slice(None))]
        for k in range(1, REACH + 1):
            total = total + w[REACH + k] * (
                ref[(*lead, pl.ds(at - k, 8), slice(None))]
                + ref[(*lead, pl.ds(at + k, 8), slice(None))]
            )
        return total

    def smooth_rows(it, slot):
        pair = order[it][slot]
        for d in (0, 1):

            def unpack(d=d):
                project_copy(it, pair, slot, d).wait_recv()
                for n in range(2):
                    proj[it, 2 * pair + n, pl.ds(0 if d == 0 else REACH + ROWS, REACH), :] = proj_in[
                        it, d, 2 * pair + n
                    ].astype(F32)

            dt, dm = SIDES[d]
            guarded(there(-dt, -dm), unpack)
        for n in range(2):
            for half in (0, 8):
                sx[pl.ds(pl.multiple_of((2 * pair + n) * ROWS + half, 8), 8), :] = taper(
                    proj, (it, 2 * pair + n), REACH + half
                )

    def column_copy(it, d, part):
        dt, dm = COLUMN_SIDES[d]
        src, dst = (pk_r, cl_in) if dm > 0 else (pk_l, cr_in)
        return pltpu.make_async_remote_copy(
            src_ref=src.at[it, part],
            dst_ref=dst.at[it, part, column_place(dt)],
            send_sem=c_send.at[it, d, part], recv_sem=c_recv.at[it, d, part],
            device_id=peer(dt, dm), device_id_type=MESH,
        )

    def column_place(dt):
        return 1 if dt == 0 else 0 if dt > 0 else 2

    def send_columns(it, part):
        rights, lefts = [], []
        for half in (0, 8):
            right = jnp.zeros((8, COLS), F32)
            left = jnp.zeros((8, COLS), F32)
            for n in range(8):
                v = proj[it, 8 * part + n, REACH + half : REACH + half + 8, :]
                right = jnp.where(group == n, pltpu.roll(v, (16 * n - 112) % COLS, 1), right)
                left = jnp.where(group == n, pltpu.roll(v, 16 * n, 1), left)
            rights.append(right)
            lefts.append(left)
        pk_r[it, part] = jnp.concatenate(rights).astype(BF16)
        pk_l[it, part] = jnp.concatenate(lefts).astype(BF16)
        for d, side in enumerate(COLUMN_SIDES):
            guarded(there(*side), column_copy(it, d, part).start)

    def receive_columns(it):
        for d, (dt, dm) in enumerate(COLUMN_SIDES):

            def unpack(d=d, dt=dt, dm=dm):
                place = column_place(dt)
                got, to = (cl_in, cl) if dm > 0 else (cr_in, cr)
                for part in range(2):
                    column_copy(it, d, part).wait_recv()
                    to[it, part, place * REACH : (place + 1) * REACH, :] = got[
                        it, part, place
                    ].astype(F32)

            guarded(there(-dt, -dm), unpack)

    def split(x):
        high = x.astype(BF16)
        return high, (x - high.astype(F32)).astype(BF16)

    def times(x, which):
        high, low = split(x)
        dot = functools.partial(jnp.dot, preferred_element_type=F32)
        return dot(high, band[which, 0]) + (dot(low, band[which, 0]) + dot(high, band[which, 1]))

    def smooth_columns(it):
        z[...] = times(sx[...], 0)
        receive_columns(it)
        outer = []
        for which, ref in ((1, cl), (2, cr)):
            x = jnp.concatenate(
                [taper(ref, (it, part), REACH + half) for part in range(2) for half in (0, 8)]
            )
            outer.append(times(x, which))
        for part in range(2):
            for half in (0, 8):
                at = part * ROWS + half
                from_left, from_right = (x[at : at + 8, :] for x in outer)
                for n in range(8):
                    to = (8 * part + n) * ROWS + half
                    z[to : to + 8, :] = z[to : to + 8, :] + jnp.where(
                        lane < 16,
                        pltpu.roll(from_left, (-16 * n) % COLS, 1),
                        jnp.where(
                            lane >= 112, pltpu.roll(from_right, (112 - 16 * n) % COLS, 1), 0.0
                        ),
                    )

    def out_copy(part):
        levels = pl.ds(part * (LEV // PARTS), LEV // PARTS)
        return pltpu.make_async_copy(half_ref.at[levels], out_hbm.at[levels], out_sem.at[part])

    def increments(it):
        width = 4

        def levels(step, carry):
            sums = [jnp.zeros((ROWS, COLS), F32) for _ in range(width)]
            for pair in range(8):
                for n in range(2):
                    v = z[pl.ds((2 * pair + n) * ROWS, ROWS), :]
                    for i in range(width):
                        sums[i] = sums[i] + mt[pair, n, width * step + i].astype(F32) * v
            for i in range(width):
                l = width * step + i
                if it == 0:
                    half = relax * sums[i]
                    half_ref[l] = half
                    v = res[l] - half
                    a1[pl.ds(HALO * LEV + l, 8, stride=LEV), :] = v[0:8]
                    a1[pl.ds((HALO + 8) * LEV + l, 8, stride=LEV), :] = v[8:16]
                else:
                    half_ref[l] = half_ref[l] + relax * sums[i]
            return carry

        parts = PARTS if it else HALVES
        for part in range(parts):
            count = LEV // parts // width
            lax.fori_loop(part * count, (part + 1) * count, levels, 0)
            if it == 0:
                send_rows(1, part)
            else:
                out_copy(part).start()

    def halos_sent(it):
        for d in (0, 1):
            for half in range(HALVES):
                guarded(there(*SIDES[d]), row_copy(it, d, half).wait_send)
        for d in range(8):
            guarded(there(*SIDES[d]), quad_copy(it, d).wait_send)

    def projects_sent(it):
        for slot in range(8):
            for d in (0, 1):
                guarded(there(*SIDES[d]), project_copy(it, order[it][slot], slot, d).wait_send)

    def columns_sent(it):
        for d, side in enumerate(COLUMN_SIDES):
            for part in range(2):
                guarded(there(*side), column_copy(it, d, part).wait_send)

    adjoint_early(0)
    adjoint_late(0)
    own_copy.wait()
    project(0, order[0][0], 0, LEV, True)
    send_project(0, 0)
    for i, c in ORDER:
        member_copy(i, c).wait_recv()
        project(0, order[0][1 + i], c * CLEV, CLEV, c == 0)
        if c == CHUNKS - 1:
            send_project(0, 1 + i)
    for part in range(2):
        send_columns(0, part)
    for slot in range(8):
        smooth_rows(0, slot)
    smooth_columns(0)
    increments(0)

    send_halos(1)
    adjoint_early(1)
    for i, c in ORDER:
        member_copy(i, c).wait_send()
    halos_sent(0)
    projects_sent(0)
    columns_sent(0)
    adjoint_late(1)
    for slot in range(8):
        if slot % 2 == 0:
            project_both(1, slot)
        send_project(1, slot)
        if slot % 4 == 3:
            send_columns(1, slot // 4)
    halos_sent(1)
    for slot in range(8):
        smooth_rows(1, slot)
    projects_sent(1)
    smooth_columns(1)
    increments(1)
    columns_sent(1)
    for part in range(PARTS):
        out_copy(part).wait()


def per_device(tiles, blocks, residual_in, members, wind_x, wind_y):
    vmem = pltpu.VMEM
    dma = lambda *shape: pltpu.SemaphoreType.DMA(shape)
    anywhere = pl.BlockSpec(memory_space=pl.ANY)
    extended = vmem((XROWS * LEV, COLS), F32)
    coefficient = vmem((LEV, COLS), F32)
    half = pl.pallas_call(
        functools.partial(kernel, tiles, blocks),
        out_shape=jax.ShapeDtypeStruct((LEV, ROWS, COLS), F32),
        in_specs=[anywhere] * 4,
        out_specs=anywhere,
        scratch_shapes=[
            vmem((LEV, ROWS, COLS), F32),
            vmem((8, 2, LEV, ROWS, COLS), BF16),
            extended, extended, extended, extended, extended,
            coefficient, coefficient, coefficient,
            vmem((2, XROWS, 8, COLS), F32),
            vmem((STEPS, XROWS, 8, COLS), F32),
            vmem((STEPS, XROWS, 8, COLS), F32),
            vmem((STEPS, XROWS * LEV, COLS), F32),
            vmem((2, 4, 8, COLS), F32), vmem((2, 4, 8, COLS), F32),
            vmem((2, 6, 8, COLS), F32), vmem((2, 6, 8, COLS), F32),
            vmem((ROWS * LEV, COLS), F32),
            vmem((LEV * ROWS, COLS), F32),
            vmem((2, 2, HALVES, HALO * HLEV, COLS), BF16),
            vmem((2, 2, HALVES, HALO * HLEV, COLS), BF16),
            vmem((2, 16, ROWS + 2 * REACH, COLS), F32),
            vmem((2, 16, ROWS, COLS), BF16),
            vmem((2, 2, 16, REACH, COLS), BF16),
            vmem((16 * ROWS, COLS), F32),
            vmem((2, 2, ROWS, COLS), BF16), vmem((2, 2, ROWS, COLS), BF16),
            vmem((2, 2, 3, REACH, COLS), BF16),
            vmem((2, 2, 3, REACH, COLS), BF16),
            vmem((2, 2, ROWS + 2 * REACH, COLS), F32),
            vmem((2, 2, ROWS + 2 * REACH, COLS), F32),
            vmem((3, 2, COLS, COLS), BF16),
            vmem((16 * ROWS, COLS), F32),
            vmem((LEV, ROWS, COLS), F32),
            pltpu.SMEM((LEV,), F32), pltpu.SMEM((LEV,), F32),
            pltpu.SemaphoreType.DMA, pltpu.SemaphoreType.DMA, dma(2), dma(PARTS),
            dma(len(FLOWS), CHUNKS), dma(len(FLOWS), CHUNKS),
            dma(2, 8), dma(2, 8),
            dma(2, 2, HALVES), dma(2, 2, HALVES),
            dma(2, 8, 2), dma(2, 8, 2),
            dma(2, len(COLUMN_SIDES), 2), dma(2, len(COLUMN_SIDES), 2),
        ],
        compiler_params=pltpu.CompilerParams(collective_id=0, has_side_effects=True),
        name="ensemble_step",
    )(residual_in, members, wind_x, wind_y)
    return (half * (1.0 / relax), residual_in - half)


def solution(mesh):
    return jax.shard_map(
        functools.partial(per_device, mesh.shape["tile"], mesh.shape["member"]),
        mesh=mesh,
        in_specs=(P(None, "tile", "member"), P("member", None, "tile", None), P(), P()),
        out_specs=(P(None, "tile", "member"), P(None, "tile", "member")),
        check_vma=False,
    )
```
